128 devices in a mesh: gx: 8 (over x_lo, z), gy: 8 (over y, core), gz: 2 (over x_hi).
Axes of the slice: x: 4 (x_hi: 2, x_lo: 2; x = x_hi * 2 + x_lo), y: 4, z: 4, core: 2. Of those that a mesh axis runs over, the one named last changes fastest.
Arguments:
- basis: bfloat16 [64, 64, 16, 8192], P('gx', 'gy', 'gz'), may hold values from -0.09375 to 0.09375
- classes: int32 [64, 64, 16], P('gx', 'gy', 'gz'), may hold values from 0 to 15
- cond_table: float32 [16], replicated, may hold values from 0.5 to 2
- ground_table: float32 [16], replicated, may hold values from 4 to 40
- port_cells: int32 [2048], replicated, may hold values from 0 to 65535
- port_load: float32 [2048], replicated, may hold values from 20 to 200
Outputs:
- reduced: float32 [8192, 1024], P(('gx', 'gz'), 'gy')
- factor: float32 [8192, 1024], P(('gx', 'gz'), 'gy')
The draws below stay inside these ranges and needn't reach their ends.
Inputs may be any that keep to these rules, and one draw needn't show every extreme that they name: `port_cells`: several ports may name the same cell; their loads add.
All inputs are finite; a program needn't handle non-finite values.
Results may differ from the reference program's by a relative error of at most 0.0024.
Values may be sent and summed in bfloat16 or wider, within the bound.
A program may use at most 256 MiB of HBM per device.

```python
import math
import jax
import jax.numpy as jnp
from jax import lax

K = 8192
NB = 512
PANELS = 2
NCLS = 16
PORTS = 2048
NX = 64
NY = 64
NZ = 16
CELLS = 65536


def touch_ends(drawn, own_key, least, largest):
    extent = drawn.shape
    spot = [jax.random.randint(jax.random.fold_in(own_key, axis), (), 0, extent[axis]) for axis in range(len(extent))]
    drawn = drawn.at[tuple(spot)].set(least)
    longest = extent.index(max(extent))
    spot[longest] = (spot[longest] + 1) % extent[longest]
    return drawn.at[tuple(spot)].set(largest)


def levels(key, dims, shards, low, largest):
    def one(position, shards_of):
        heights = jax.random.uniform(jax.random.fold_in(jax.random.fold_in(key, 6), position), (shards_of,), jnp.float32, low / len(shards), largest / len(shards))
        return jnp.repeat(jnp.exp(heights), dims[position] // shards_of).reshape((-1,) + (1,) * (len(dims) - position - 1))

    loudness = one(*shards[0])
    for cut in shards[1:]:
        loudness = loudness * one(*cut)
    return loudness


def bell_draw(stream_key, extent, spread, limit, shards=(), kind=jnp.bfloat16):
    values = spread * jax.random.normal(stream_key, extent, jnp.float32)
    if shards:
        values = values * levels(stream_key, extent, shards, -0.22, 0.18)
    return jnp.clip(values, -limit, limit).astype(kind)


def setup_inputs(seed: int = 0) -> dict:
    streams_of = jax.random.split(jax.random.key(seed), 7)
    return {
        "basis": bell_draw(streams_of[0], (NX, NY, NZ, K), (CELLS // 16) ** -0.5, 0.09375, ((0, 8), (1, 8), (2, 2))),
        "classes": touch_ends(jax.random.randint(streams_of[1], (NX, NY, NZ), 0, NCLS), jax.random.fold_in(streams_of[1], 1), 0, NCLS - 1).astype(jnp.int32),
        "cond_table": jnp.clip(jnp.exp(jax.random.uniform(streams_of[2], (NCLS,), jnp.float32, math.log(0.5), math.log(2.0))), 0.5, 2.0),
        "ground_table": jnp.clip(jnp.exp(jax.random.uniform(streams_of[3], (NCLS,), jnp.float32, math.log(4.0), math.log(40.0))), 4.0, 40.0),
        "port_cells": touch_ends(jax.random.randint(streams_of[4], (PORTS,), 0, CELLS), jax.random.fold_in(streams_of[4], 1), 0, CELLS - 1).astype(jnp.int32),
        "port_load": jnp.clip(jnp.exp(jax.random.uniform(streams_of[5], (PORTS,), jnp.float32, math.log(20.0), math.log(200.0))), 20.0, 200.0),
    }


def lead_factor(leading, panel_width, panel_total):
    result = jnp.zeros(leading.shape, jnp.float32)
    row_ids = jnp.arange(leading.shape[0], dtype=jnp.int32)
    diagonals = []
    for panel_index in range(panel_total):
        begin_col = panel_index * panel_width
        block_part = leading[:, begin_col:begin_col + panel_width]
        if panel_index > 0:
            block_part = block_part - jnp.dot(result[:, :begin_col], result[begin_col:begin_col + panel_width, :begin_col].T, precision=lax.Precision.HIGHEST)
        diagonal = jnp.linalg.cholesky(block_part[begin_col:begin_col + panel_width])
        solved = jax.scipy.linalg.solve_triangular(diagonal, block_part.T, lower=True).T
        column_ids = begin_col + jnp.arange(panel_width, dtype=jnp.int32)
        solved = jnp.where(column_ids[None, :] <= row_ids[:, None], solved, jnp.float32(0.0))
        result = result.at[:, begin_col:begin_col + panel_width].set(solved)
        diagonals.append(diagonal)
    return (result, diagonals)

def rows_factor(matrix_rows, offset, lead_l, diagonals, panel_width):
    result = jnp.zeros(matrix_rows.shape, jnp.float32)
    row_ids = offset + jnp.arange(matrix_rows.shape[0], dtype=jnp.int32)
    for panel_index in range(len(diagonals)):
        begin_col = panel_index * panel_width
        block_part = matrix_rows[:, begin_col:begin_col + panel_width]
        if panel_index > 0:
            block_part = block_part - jnp.dot(result[:, :begin_col], lead_l[begin_col:begin_col + panel_width, :begin_col].T, precision=lax.Precision.HIGHEST)
        solved = jax.scipy.linalg.solve_triangular(diagonals[panel_index], block_part.T, lower=True).T
        column_ids = begin_col + jnp.arange(panel_width, dtype=jnp.int32)
        solved = jnp.where(column_ids[None, :] <= row_ids[:, None], solved, jnp.float32(0.0))
        result = result.at[:, begin_col:begin_col + panel_width].set(solved)
    return result

def reference(basis, classes, cond_table, ground_table, port_cells, port_load):
    panel_cols = PANELS * NB
    conduct = cond_table[classes]
    terminal = jax.ops.segment_sum(port_load, port_cells, num_segments=CELLS).reshape(NX, NY, NZ)
    grounds = ground_table[classes] + terminal
    panel_part = basis[:, :, :, :panel_cols].astype(jnp.float32)
    scaled = (conduct[..., None] * panel_part).astype(jnp.bfloat16)
    scaled_wide = scaled.astype(jnp.float32)
    padded = jnp.pad(scaled_wide, ((1, 1), (1, 1), (1, 1), (0, 0)))
    beside = padded[2:, 1:-1, 1:-1] + padded[:-2, 1:-1, 1:-1]
    beside = beside + padded[1:-1, 2:, 1:-1] + padded[1:-1, :-2, 1:-1]
    beside = beside + padded[1:-1, 1:-1, 2:] + padded[1:-1, 1:-1, :-2]
    image_full = (conduct[..., None] * (6.0 * scaled_wide - beside) + grounds[..., None] * panel_part).astype(jnp.bfloat16)
    reduced = lax.dot_general(basis.reshape(CELLS, K).astype(jnp.float32), image_full.reshape(CELLS, panel_cols).astype(jnp.float32), (((0,), (0,)), ((), ())), preferred_element_type=jnp.float32)
    lead_l, diagonals = lead_factor(reduced[:panel_cols], NB, PANELS)
    factor = rows_factor(reduced, 0, lead_l, diagonals, NB)
    return (reduced, factor)
```

```python
import jax
import jax.numpy as jnp
from jax import lax
from jax.experimental import pallas as pl
from jax.experimental.pallas import tpu as pltpu
from jax.sharding import PartitionSpec as P

NB = 512
PANELS = 2
COLS = NB * PANELS
F32 = jnp.float32
BF16 = jnp.bfloat16
HI = lax.Precision.HIGHEST
MESH = pl.DeviceIdType.MESH


def here():
    gx, gy, gz = lax.axis_index("gx"), lax.axis_index("gy"), lax.axis_index("gz")
    return gz * 2 + gx // 4, gy // 2, gx % 4, gy % 2


def device(x, y, z, core):
    return ((x % 2) * 4 + z, y * 2 + core, x // 2)


def along(axis, pos, place):
    x, y, z, core = place
    if axis == "x":
        x = pos
    elif axis == "y":
        y = pos
    else:
        z = pos
    return device(x, y, z, core)


def position(axis, place):
    return place["xyz".index(axis)]


def greet(devices):
    barrier = pltpu.get_barrier_semaphore()
    for dev in devices:
        pl.semaphore_signal(barrier, inc=1, device_id=dev, device_id_type=MESH)
    pl.semaphore_wait(barrier, len(devices))


def torus_peers(place):
    x, y, z, core = place
    peers = []
    for axis in "xyz":
        pos = position(axis, place)
        peers += [along(axis, (pos + 1) % 4, place), along(axis, (pos + 3) % 4, place)]
    return peers + [device(x, y, z, 1 - core)]


class Wires:
    def __init__(self, send_sem, recv_sem):
        self.send_sem, self.recv_sem, self.used = send_sem, recv_sem, 0

    def take(self, count=1):
        self.used += count
        return self.used - count

    def copy(self, number, src, dst, dev):
        return pltpu.make_async_remote_copy(
            src_ref=src,
            dst_ref=dst,
            send_sem=self.send_sem.at[number],
            recv_sem=self.recv_sem.at[number],
            device_id=dev,
            device_id_type=MESH,
        )

    def send(self, number, src, dst, dev):
        copy = self.copy(number, src, dst, dev)
        copy.start()
        return copy


def each(dims, body):
    count = 4 ** len(dims)
    if count == 1:
        body(())
        return

    def step(i, _):
        body(tuple((i // 4 ** (len(dims) - 1 - d)) % 4 for d in range(len(dims))))
        return 0

    lax.fori_loop(0, count, step, 0)


def put(index, dims, axis, pos):
    index = list(index)
    index.insert(dims.index(axis), pos)
    return tuple(index)


class Reduce:
    def __init__(self, place, wires, axis, dims, home, out, rows, lane, got):
        self.axis, self.dims, self.home, self.out, self.rows, self.got = axis, dims, home, out, rows, got
        self.first, self.second = pl.ds(lane, 128), pl.ds(lane + 128, 128)
        self.rest = tuple(d for d in dims if d != axis)
        self.wires, self.base = wires, wires.take(6)
        me = position(axis, place)
        self.me, self.plus, self.minus, self.opposite = me, (me + 1) % 4, (me + 3) % 4, (me + 2) % 4
        self.up, self.down = along(axis, self.plus, place), along(axis, self.minus, place)
        self.copies = {}

    def go(self, slot, pos, lanes, dev):
        index = put([pl.ds(0, 4)] * len(self.rest), self.dims, self.axis, pos)
        src = self.out.at[index + (self.rows, lanes)]
        self.copies[slot] = self.wires.send(self.base + slot, src, self.got.at[slot], dev)

    def begin(self):
        self.go(0, self.opposite, self.first, self.up)
        self.go(3, self.opposite, self.second, self.down)
        self.go(1, self.plus, self.second, self.up)
        self.go(4, self.minus, self.first, self.down)

    def relay(self):
        for slot, pos, lanes, dev in (
            (0, self.plus, self.first, self.up),
            (3, self.minus, self.second, self.down),
        ):
            self.copies[slot].wait_recv()

            def body(index):
                at = put(index, self.dims, self.axis, pos) + (self.rows, lanes)
                total = self.home[at] + self.got[(slot,) + index].astype(F32)
                self.out[at] = total.astype(self.out.dtype)

            each(self.rest, body)
            self.go(slot + 2, pos, lanes, dev)

    def finish(self, store):
        for slot in (1, 4, 2, 5):
            self.copies[slot].wait_recv()

        def body(index):
            for half, lanes, one, two in ((0, self.first, 2, 4), (1, self.second, 1, 5)):
                at = put(index, self.dims, self.axis, self.me) + (self.rows, lanes)
                total = self.home[at] + self.got[(one,) + index].astype(F32)
                store(index, half, total + self.got[(two,) + index].astype(F32))

        each(self.rest, body)
        for copy in self.copies.values():
            copy.wait_send()


class Gather:
    def __init__(self, place, wires, axis, ref, base, size, lanes, halves, mate=None):
        self.ref, self.base, self.size, self.mate = ref, base, size, mate
        self.lanes, self.halves = lanes, halves
        self.wires, self.first = wires, wires.take(8)
        me = position(axis, place)
        self.me, self.plus, self.minus, self.opposite = me, (me + 1) % 4, (me + 3) % 4, (me + 2) % 4
        self.up, self.down = along(axis, self.plus, place), along(axis, self.minus, place)
        self.copies = []
        self.passed = []

    def go(self, slot, pos, lanes, dev):
        rows = pl.ds(pl.multiple_of(self.base + pos * self.size, self.size), self.size)
        part = self.ref.at[rows, lanes]
        return self.wires.send(self.first + slot, part, part, dev)

    def share(self, slot, pos):
        if self.mate is not None:
            self.passed.append(self.go(slot, pos, self.lanes, self.mate))

    def begin(self):
        self.copies += [self.go(0, self.me, self.lanes, self.up)]
        self.copies += [self.go(1, self.me, self.lanes, self.down)]
        self.share(4, self.me)

    def relay(self):
        self.copies[0].wait_recv()
        self.copies += [self.go(2, self.minus, self.halves[0], self.up)]
        self.copies[1].wait_recv()
        self.copies += [self.go(3, self.plus, self.halves[1], self.down)]
        self.share(5, self.minus)
        self.share(6, self.plus)

    def arrive(self):
        self.copies[2].wait_recv()
        self.copies[3].wait_recv()
        self.share(7, self.opposite)

    def finish(self):
        for copy in self.passed:
            copy.wait_recv()
        for copy in self.copies + self.passed:
            copy.wait_send()


def row_of(block, k):
    return jnp.broadcast_to(block[k : k + 1, :], block.shape)


def eliminate(rows, right, cols, sub):
    scale = jnp.zeros((8, 128), F32)
    for k in range(8):
        inv = 1.0 / row_of(cols[0][k], k)
        scale = jnp.where(sub == k, inv, scale)
        pivot_row = row_of(rows[0], k)
        pivot_right = row_of(right[0], k)
        heads = [row_of(cols[0][m], k) for m in range(k + 1, 8)]
        for t in range(len(rows)):
            mult = cols[t][k] * inv
            if t == 0:
                mult = jnp.where(sub > k, mult, 0.0)
            for i, m in enumerate(range(k + 1, 8)):
                cols[t][m] = cols[t][m] - mult * heads[i]
            rows[t] = rows[t] - mult * pivot_row
            right[t] = right[t] - mult * pivot_right
    return rows, right, scale


def factor_block(a_ref, x_ref, middle):
    sub = lax.broadcasted_iota(jnp.int32, (8, 128), 0)
    row = lax.broadcasted_iota(jnp.int32, (128, 128), 0)
    lane = lax.broadcasted_iota(jnp.int32, (128, 128), 1)
    x_ref[...] = jnp.where(row == lane, 1.0, 0.0).astype(F32)
    for g in range(16):
        if g == 8:
            middle()
        b = g * 8
        n = 2 if g < 15 else 1
        rows = [a_ref[b + 8 * t : b + 8 * t + 8, :] for t in range(n)]
        right = [x_ref[b + 8 * t : b + 8 * t + 8, :] for t in range(n)]
        cols = [
            [jnp.broadcast_to(rows[t][:, b + m : b + m + 1], (8, 128)) for m in range(8)]
            for t in range(n)
        ]
        rows, right, scale = eliminate(rows, right, cols, sub)
        if n == 2:
            a_ref[b + 8 : b + 16, :] = rows[1]
            x_ref[b + 8 : b + 16, :] = right[1]
        if g < 14:
            low = b + 16
            left = rows[0] * scale
            both = jnp.concatenate([rows[0], right[0]], axis=1)
            change = lax.dot_general(
                left, both, (((0,), (0,)), ((), ())), precision=HI, preferred_element_type=F32
            )
            a_ref[low:, :] = a_ref[low:, :] - change[low:, :128]
            x_ref[low:, :] = x_ref[low:, :] - change[low:, 128:]
        x_ref[b : b + 8, :] = right[0] * jnp.sqrt(scale)


def invert_factor(work, a_ref, x_ref, between):
    n = work.shape[0]
    for k in range(n // 128):
        b, e = k * 128, k * 128 + 128
        a_ref[...] = work[b:e, b:e]
        factor_block(a_ref, x_ref, between)
        inverse = x_ref[...]
        work[b:e, b:e] = inverse
        for low, high in ((0, b), (e, n)):
            if low < high:
                work[b:e, low:high] = jnp.dot(
                    inverse, work[b:e, low:high], precision=HI, preferred_element_type=F32
                )
        if e < n:
            change = lax.dot_general(
                work[b:e, e:],
                work[b:e, :],
                (((0,), (0,)), ((), ())),
                precision=HI,
                preferred_element_type=F32,
            )
            if b:
                work[e:, :b] = work[e:, :b] - change[:, :b]
            work[e:, b:e] = -change[:, b:e]
            work[e:, e:] = work[e:, e:] - change[:, e:]
        between()


DIMS = "xzy"
ORDERS = ("xyz", "yzx", "zxy")
LEAD_ORDERS = ("xyz", "yzx")
PARTS = ((0, 96), (96, 80), (176, 80))
EVERY = slice(None)
CHUNKS = COLS // 128


def kernel(
    basis, cond, ground, tile, factor, other,
    panel, scaled, faces, halos, hz, image, image_t,
    lead_window, lead_home, lead_out, window, home, out, work, a_ref, x_ref, total, rows_t,
    *rest,
):
    lead_gots, lead_sums, gots, sums = rest[:6], rest[6:10], rest[10:19], rest[19:25]
    load_sem, send_sem, recv_sem = rest[25:]
    wires = Wires(send_sem, recv_sem)
    gx, gy, gz = lax.axis_index("gx"), lax.axis_index("gy"), lax.axis_index("gz")
    place = here()
    x, y, z, core = place
    mate = device(x, y, z, 1 - core)
    beside = [
        ((gx + 7) % 8, gy, gz),
        ((gx + 1) % 8, gy, gz),
        (gx, (gy + 7) % 8, gz),
        (gx, (gy + 1) % 8, gz),
        (gx, gy, 1 - gz),
    ]
    load = pltpu.make_async_copy(basis.at[:, pl.ds(0, COLS)], panel, load_sem.at[0])
    load.start()
    own_lead = []
    for rb in range(2):
        begin = pl.multiple_of(rb * 512 + core * 256, 256)
        own_lead.append(
            pltpu.make_async_copy(
                basis.at[:, pl.ds(begin, 256)],
                lead_window.at[pl.ds(0, 512), pl.ds(rb * 256, 256)],
                load_sem.at[1 + rb],
            )
        )
        own_lead[rb].start()
    greet(beside + torus_peers(place))

    swap_base = wires.take(16)

    def swap(rb, dst):
        begin = pl.multiple_of(rb * 512 + (1 - core) * 256, 256)
        return wires.copy(swap_base + rb, basis.at[:, pl.ds(begin, 256)], dst, mate)

    def far(rb):
        return other.at[:, pl.ds(pl.multiple_of(rb * 256, 256), 256)]

    lead_swaps = [
        swap(rb, lead_window.at[pl.ds(512, 512), pl.ds(rb * 256, 256)]) for rb in range(2)
    ]
    for copy in lead_swaps:
        copy.start()
    load.wait()

    def scale(c, _):
        lanes = pl.ds(pl.multiple_of(c * 128, 128), 128)
        inner = lax.broadcasted_iota(jnp.int32, (8, 128), 0)
        y_low, y_high, z_face = [], [], []
        for i in range(8):
            rows = pl.ds(i * 64, 64)
            value = (cond[rows, :] * panel[rows, lanes].astype(F32)).astype(BF16)
            scaled[rows, lanes] = value
            if i == 0:
                faces[0, :, lanes] = value
            if i == 7:
                faces[1, :, lanes] = value
            value = value.astype(F32)
            y_low.append(value[:8])
            y_high.append(value[56:])
            face = jnp.zeros((8, 128), F32)
            for j in range(8):
                cell = value[j * 8 : j * 8 + 8]
                low = jnp.broadcast_to(cell[0:1, :], (8, 128))
                high = jnp.broadcast_to(cell[7:8, :], (8, 128))
                face = jnp.where(inner == j, jnp.where(gz == 1, low, high), face)
            z_face.append(face)
        for f, face in ((2, y_low), (3, y_high), (4, z_face)):
            faces[f, :, lanes] = jnp.concatenate(face, axis=0).astype(BF16)
        return 0

    lax.fori_loop(0, CHUNKS, scale, 0)
    lands = [1, 0, 3, 2, 4]
    face_base = wires.take(5)
    face_copies = [
        wires.send(face_base + f, faces.at[f], halos.at[lands[f]], beside[f]) for f in range(5)
    ]

    def start_swap(rb, _):
        swap(rb, far(rb)).start()
        return 0

    lax.fori_loop(2, 16, start_swap, 0)
    for copy in face_copies:
        copy.wait()

    keep = [gx > 0, gx < 7, gy > 0, gy < 7]
    image_base = wires.take(CHUNKS)

    def image_copy(c):
        lanes = pl.ds(pl.multiple_of(c * 128, 128), 128)
        return wires.copy(
            image_base + c, image.at[pl.ds(0, 512), lanes], image.at[pl.ds(512, 512), lanes], mate
        )

    def stencil(c, _):
        lanes = pl.ds(pl.multiple_of(c * 128, 128), 128)
        inner = lax.broadcasted_iota(jnp.int32, (64, 128), 0) % 8

        def halo(f):
            return jnp.where(keep[f], halos[f, :, lanes].astype(F32), 0.0)

        hz[...] = halos[4, :, lanes].astype(F32)
        x_low, x_high, y_low, y_high = halo(0), halo(1), halo(2), halo(3)
        for i in range(8):
            rows = pl.ds(i * 64, 64)
            me = scaled[rows, lanes].astype(F32)
            down = scaled[pl.ds((i - 1) * 64, 64), lanes].astype(F32) if i > 0 else x_low
            up = scaled[pl.ds((i + 1) * 64, 64), lanes].astype(F32) if i < 7 else x_high
            around = up + down
            around = around + jnp.concatenate([me[8:], y_high[i * 8 : i * 8 + 8]], axis=0)
            around = around + jnp.concatenate([y_low[i * 8 : i * 8 + 8], me[:56]], axis=0)
            ends = jnp.concatenate(
                [jnp.broadcast_to(hz[i * 8 + j : i * 8 + j + 1, :], (8, 128)) for j in range(8)],
                axis=0,
            )
            high = pltpu.roll(me, 63, 0)
            low = pltpu.roll(me, 1, 0)
            high = jnp.where(inner == 7, jnp.where(gz == 0, ends, 0.0), high)
            low = jnp.where(inner == 0, jnp.where(gz == 1, ends, 0.0), low)
            around = around + high + low
            value = cond[rows, :] * (6.0 * me - around)
            value = value + ground[rows, :] * panel[rows, lanes].astype(F32)
            image[rows, lanes] = value.astype(BF16)
        image_copy(c).start()
        return 0

    lax.fori_loop(0, CHUNKS, stencil, 0)

    def turn(c, _):
        image_copy(c).wait()
        rows = pl.ds(pl.multiple_of(c * 128, 128), 128)
        image_t[rows, :] = image[:, rows].T
        return 0

    lax.fori_loop(0, CHUNKS, turn, 0)

    for copy in own_lead + lead_swaps:
        copy.wait()

    def lead_terms(c, _):
        rows = pl.ds(pl.multiple_of(c * 256, 256), 256)
        product = jnp.dot(image_t[rows, :], lead_window[...], preferred_element_type=F32)
        for i in range(16):
            value = product[i * 16 : i * 16 + 16, :]
            lead_home[c, i // 4, i % 4] = value
            lead_out[c, i // 4, i % 4] = value.astype(BF16)
        return 0

    lax.fori_loop(0, 4, lead_terms, 0)

    def fetch(rb):
        slot = rb % 2
        begin = pl.multiple_of(rb * 512 + core * 256, 256)
        return (
            pltpu.make_async_copy(
                basis.at[:, pl.ds(begin, 256)],
                window.at[slot, pl.ds(0, 512), :],
                load_sem.at[3 + slot],
            ),
            pltpu.make_async_copy(
                far(rb), window.at[slot, pl.ds(512, 512), :], load_sem.at[5 + slot]
            ),
        )

    def start_fetch(rb):
        swap(rb, far(rb)).wait()
        for copy in fetch(rb):
            copy.start()

    def multiply(rb, read):
        to_x, to_z = (rb % 2) * 2 + rb // 8, (rb // 2) % 4

        def one(c, _):
            rows = pl.ds(pl.multiple_of(c * 256, 256), 256)
            product = jnp.dot(image_t[rows, :], read(), preferred_element_type=F32)
            home[to_x, to_z, c] = product
            out[to_x, to_z, c] = product.astype(BF16)
            return 0

        lax.fori_loop(0, 4, one, 0)

    def terms(low, high):
        def one(rb, _):
            for copy in fetch(rb):
                copy.wait()

            @pl.when(rb < 15)
            def _():
                start_fetch(rb + 1)

            multiply(rb, lambda: window[rb % 2])
            return 0

        lax.fori_loop(low, high, one, 0)

    def lead_block(rb):
        multiply(rb, lambda: lead_window[:, rb * 256 : rb * 256 + 256])

    dims = [LEAD_ORDERS[p] for p in range(2)]
    homes, outs, lane = [lead_home] * 2, [lead_out] * 2, [0, 256]
    for stage in range(3):
        steps = [
            Reduce(
                place, wires, LEAD_ORDERS[p][stage], dims[p], homes[p], outs[p], EVERY, lane[p],
                lead_gots[p * 3 + stage],
            )
            for p in range(2)
        ]
        for step in steps:
            step.begin()
        if stage == 0:
            start_fetch(2)
            lead_block(0)
            lead_block(1)
        else:
            terms(5 * stage, 5 * stage + 2)
        for step in steps:
            step.relay()
        if stage == 0:
            terms(2, 5)
        else:
            terms(5 * stage + 2, 5 * stage + 5)
        for p, step in enumerate(steps):
            if stage < 2:
                acc = lead_sums[p * 2 + stage]

                def store(index, half, value, acc=acc):
                    acc[index + (EVERY, pl.ds(half * 128, 128))] = value

                homes[p] = outs[p] = acc
                lane[p] = 0
            else:
                at = [position(axis, place) for axis in LEAD_ORDERS[p]]
                rows = pl.ds(pl.multiple_of((at[0] * 16 + at[1] * 4 + at[2]) * 16, 16), 16)

                def store(index, half, value, p=p, rows=rows):
                    begin = pl.multiple_of(p * 512 + core * 256 + half * 128, 128)
                    work[rows, pl.ds(begin, 128)] = value

            step.finish(store)
            dims[p] = step.rest
    for stage in range(3):
        steps = []
        for p in range(2):
            at = [position(axis, place) for axis in LEAD_ORDERS[p]]
            base = (at[0] * 256 + at[1] * 64, at[0] * 256, 0)[stage]
            begin = pl.multiple_of(p * 512 + core * 256, 256)
            halves = [pl.ds(begin, 128), pl.ds(pl.multiple_of(begin + 128, 128), 128)]
            steps.append(
                Gather(
                    place, wires, LEAD_ORDERS[p][2 - stage], work, base, (16, 64, 256)[stage],
                    pl.ds(begin, 256), halves, mate if stage == 2 else None,
                )
            )
        for step in steps:
            step.begin()
        if stage == 0:
            terms(15, 16)
        for step in steps:
            step.relay()
        if stage < 2:
            for step in steps:
                step.arrive()
                step.finish()

    def gather_rows():
        slots = [2 * ((y + d) % 4) + core for d in range(4)]
        up, down = along("y", (y + 1) % 4, place), along("y", (y + 3) % 4, place)
        base = wires.take(8)

        def go(number, slot, lanes, dev):
            block = rows_t.at[pl.ds(pl.multiple_of(slot * 128, 128), 128), lanes]
            return wires.send(base + number, block, block, dev)

        whole, low, high = pl.ds(0, 512), pl.ds(0, 256), pl.ds(256, 256)
        one, two = go(0, slots[0], whole, up), go(1, slots[0], whole, down)
        passed = [go(4, slots[0], whole, mate)]
        yield
        one.wait_recv()
        three = go(2, slots[3], low, up)
        passed += [go(5, slots[3], whole, mate)]
        two.wait_recv()
        four = go(3, slots[1], high, down)
        passed += [go(6, slots[1], whole, mate)]
        yield
        three.wait_recv()
        four.wait_recv()
        passed += [go(7, slots[2], whole, mate)]
        for copy in passed:
            copy.wait_recv()
        for copy in passed + [one, two, three, four]:
            copy.wait_send()

    def all_rows():
        dims, rows = [DIMS] * 3, [pl.ds(begin, size) for begin, size in PARTS]
        homes, outs = [home] * 3, [out] * 3
        for stage in range(3):
            steps = [
                Reduce(
                    place, wires, ORDERS[p][stage], dims[p], homes[p], outs[p], rows[p], 0,
                    gots[p * 3 + stage],
                )
                for p in range(3)
            ]
            for step in steps:
                step.begin()
            yield
            for step in steps:
                step.relay()
            yield
            for p, step in enumerate(steps):
                if stage < 2:
                    acc = sums[p * 2 + stage]

                    def store(index, half, value, acc=acc):
                        acc[index + (EVERY, pl.ds(half * 128, 128))] = value

                    homes[p] = outs[p] = acc
                    rows[p] = EVERY
                else:

                    def store(index, half, value, p=p):
                        total[pl.ds(*PARTS[p]), pl.ds(half * 128, 128)] = value

                step.finish(store)
                dims[p] = step.rest
        mine = pl.ds(pl.multiple_of(core * 128, 128), 128)
        theirs = pl.ds(pl.multiple_of((1 - core) * 128, 128), 128)
        lanes = pl.ds(pl.multiple_of(core * 256, 256), 256)
        swapped = wires.send(wires.take(), total.at[theirs, :], tile.at[:, lanes], mate)
        tile[:, lanes] = total[mine, :]
        yield
        swapped.wait()
        rows_t[pl.ds(pl.multiple_of(gy * 128, 128), 128), :] = tile[...]
        yield from gather_rows()

    events = all_rows()
    next(events)
    for step in steps:
        step.arrive()
    for step in steps:
        step.finish()
    for b in range(0, COLS, NB):
        block = work[b : b + NB, b : b + NB]
        work[b : b + NB, b : b + NB] = 0.5 * (block + block.T)
    count = [0]

    def between():
        count[0] += 1
        if count[0] in WHEN:
            next(events)

    invert_factor(work, a_ref, x_ref, between)
    for _ in events:
        pass
    block = work[pl.ds(pl.multiple_of(gy * 128, 128), 128), :]
    lane = lax.broadcasted_iota(jnp.int32, block.shape, 1)
    block = jnp.where(lane < (gy + 1) * 128, block, 0.0)
    mine = jnp.dot(block, rows_t[...], precision=HI, preferred_element_type=F32)
    column = gy * 128 + lax.broadcasted_iota(jnp.int32, mine.shape, 0)
    row = (gx * 2 + gz) * 512 + lax.broadcasted_iota(jnp.int32, mine.shape, 1)
    factor[...] = jnp.where(column <= row, mine, 0.0).T


WHEN = (3, 8, 10, 13, 14, 15, 16)
WIRES = 180


def project(basis, cond, ground):
    any_spec = pl.BlockSpec(memory_space=pltpu.HBM)
    vmem = pl.BlockSpec(memory_space=pltpu.VMEM)
    lead_gots, lead_sums, gots, sums = [], [], [], []
    for _ in range(2):
        lead_gots += [
            pltpu.VMEM((6, 4, 4, 16, 128), BF16),
            pltpu.VMEM((6, 4, 16, 128), F32),
            pltpu.VMEM((6, 16, 128), F32),
        ]
        lead_sums += [pltpu.VMEM((4, 4, 16, 256), F32), pltpu.VMEM((4, 16, 256), F32)]
    for _, size in PARTS:
        gots += [
            pltpu.VMEM((6, 4, 4, size, 128), BF16),
            pltpu.VMEM((6, 4, size, 128), F32),
            pltpu.VMEM((6, size, 128), F32),
        ]
        sums += [pltpu.VMEM((4, 4, size, 256), F32), pltpu.VMEM((4, size, 256), F32)]
    return pl.pallas_call(
        kernel,
        out_shape=(
            jax.ShapeDtypeStruct((128, 512), F32),
            jax.ShapeDtypeStruct((512, 128), F32),
            jax.ShapeDtypeStruct((512, 4096), BF16),
        ),
        in_specs=[any_spec, vmem, vmem],
        out_specs=(vmem, vmem, any_spec),
        scratch_shapes=[
            pltpu.VMEM((512, COLS), BF16),
            pltpu.VMEM((512, COLS), BF16),
            pltpu.VMEM((5, 64, COLS), BF16),
            pltpu.VMEM((5, 64, COLS), BF16),
            pltpu.VMEM((64, 128), F32),
            pltpu.VMEM((1024, COLS), BF16),
            pltpu.VMEM((COLS, 1024), BF16),
            pltpu.VMEM((1024, 512), BF16),
            pltpu.VMEM((4, 4, 4, 16, 512), F32),
            pltpu.VMEM((4, 4, 4, 16, 512), BF16),
            pltpu.VMEM((2, 1024, 256), BF16),
            pltpu.VMEM((4, 4, 4, 256, 256), F32),
            pltpu.VMEM((4, 4, 4, 256, 256), BF16),
            pltpu.VMEM((COLS, COLS), F32),
            pltpu.VMEM((128, 128), F32),
            pltpu.VMEM((128, 128), F32),
            pltpu.VMEM((256, 256), F32),
            pltpu.VMEM((COLS, 512), F32),
            *lead_gots,
            *lead_sums,
            *gots,
            *sums,
            pltpu.SemaphoreType.DMA((7,)),
            pltpu.SemaphoreType.DMA((WIRES,)),
            pltpu.SemaphoreType.DMA((WIRES,)),
        ],
        compiler_params=pltpu.CompilerParams(
            collective_id=0, has_side_effects=True, vmem_limit_bytes=67043328
        ),
        name="project",
    )(basis, cond, ground)


def local(basis, classes, cond_table, ground_table, port_cells, port_load):
    cells_x, cells_y, cells_z, width = basis.shape
    cells = cells_x * cells_y * cells_z
    place = [
        lax.axis_index(axis) * size + jnp.arange(size, dtype=jnp.int32)
        for axis, size in (("gx", cells_x), ("gy", cells_y), ("gz", cells_z))
    ]
    total_y, total_z = cells_y * lax.axis_size("gy"), cells_z * lax.axis_size("gz")
    flat_ids = (
        (place[0][:, None, None] * total_y + place[1][None, :, None]) * total_z
        + place[2][None, None, :]
    ).reshape(cells)
    flat_classes = classes.reshape(cells)
    onehot = (flat_classes[:, None] == jnp.arange(16, dtype=jnp.int32)).astype(F32)
    conduct = jnp.sum(onehot * cond_table, axis=1)
    grounds = jnp.sum(onehot * ground_table, axis=1)
    matches = flat_ids[:, None] == port_cells[None, :]
    grounds = grounds + jnp.sum(jnp.where(matches, port_load[None, :], 0.0), axis=1)
    cond = jnp.broadcast_to(conduct[:, None], (cells, 128))
    ground = jnp.broadcast_to(grounds[:, None], (cells, 128))
    flat = basis.reshape(cells, width)
    tile, factor, _ = project(flat, cond, ground)
    return tile.T, factor


def solution(mesh):
    placed = (P("gx", "gy", "gz", None), P("gx", "gy", "gz"), P(), P(), P(), P())
    return jax.shard_map(
        local,
        mesh=mesh,
        in_specs=placed,
        out_specs=(P(("gx", "gz"), "gy"), P(("gx", "gz"), "gy")),
        check_vma=False,
    )
```

```python
import jax
import jax.numpy as jnp
from jax import lax
from jax.experimental import pallas as pl
from jax.experimental.pallas import tpu as pltpu
from jax.sharding import PartitionSpec as P

NB = 512
PANELS = 2
COLS = NB * PANELS
F32 = jnp.float32
BF16 = jnp.bfloat16
MESH = pl.DeviceIdType.MESH


def here():
    gx, gy, gz = lax.axis_index("gx"), lax.axis_index("gy"), lax.axis_index("gz")
    return gz * 2 + gx // 4, gy // 2, gx % 4, gy % 2


def device(x, y, z, core):
    return ((x % 2) * 4 + z, y * 2 + core, x // 2)


def along(axis, pos, place):
    x, y, z, core = place
    if axis == "x":
        x = pos
    elif axis == "y":
        y = pos
    else:
        z = pos
    return device(x, y, z, core)


def position(axis, place):
    return place["xyz".index(axis)]


def greet(devices):
    barrier = pltpu.get_barrier_semaphore()
    for dev in devices:
        pl.semaphore_signal(barrier, inc=1, device_id=dev, device_id_type=MESH)
    pl.semaphore_wait(barrier, len(devices))


def torus_peers(place):
    x, y, z, core = place
    peers = []
    for axis in "xyz":
        pos = position(axis, place)
        peers += [along(axis, (pos + 1) % 4, place), along(axis, (pos + 3) % 4, place)]
    return peers + [device(x, y, z, 1 - core)]


class Wires:
    def __init__(self, send_sem, recv_sem):
        self.send_sem, self.recv_sem, self.used = send_sem, recv_sem, 0

    def take(self, count=1):
        self.used += count
        return self.used - count

    def copy(self, number, src, dst, dev):
        return pltpu.make_async_remote_copy(
            src_ref=src,
            dst_ref=dst,
            send_sem=self.send_sem.at[number],
            recv_sem=self.recv_sem.at[number],
            device_id=dev,
            device_id_type=MESH,
        )

    def send(self, number, src, dst, dev):
        copy = self.copy(number, src, dst, dev)
        copy.start()
        return copy


def each(dims, body):
    count = 4 ** len(dims)
    if count == 1:
        body(())
        return

    def step(i, _):
        body(tuple((i // 4 ** (len(dims) - 1 - d)) % 4 for d in range(len(dims))))
        return 0

    lax.fori_loop(0, count, step, 0)


def put(index, dims, axis, pos):
    index = list(index)
    index.insert(dims.index(axis), pos)
    return tuple(index)


class Reduce:
    def __init__(self, place, wires, axis, dims, home, out, rows, lane, got):
        self.axis, self.dims, self.home, self.out, self.rows, self.got = axis, dims, home, out, rows, got
        self.first, self.second = pl.ds(lane, 128), pl.ds(lane + 128, 128)
        self.rest = tuple(d for d in dims if d != axis)
        self.wires, self.base = wires, wires.take(6)
        me = position(axis, place)
        self.me, self.plus, self.minus, self.opposite = me, (me + 1) % 4, (me + 3) % 4, (me + 2) % 4
        self.up, self.down = along(axis, self.plus, place), along(axis, self.minus, place)
        self.copies = {}

    def go(self, slot, pos, lanes, dev):
        index = put([pl.ds(0, 4)] * len(self.rest), self.dims, self.axis, pos)
        src = self.out.at[index + (self.rows, lanes)]
        self.copies[slot] = self.wires.send(self.base + slot, src, self.got.at[slot], dev)

    def begin(self):
        self.go(0, self.opposite, self.first, self.up)
        self.go(3, self.opposite, self.second, self.down)

    def follow(self):
        self.go(1, self.plus, self.second, self.up)
        self.go(4, self.minus, self.first, self.down)

    def relay(self):
        for slot, pos, lanes, dev in (
            (0, self.plus, self.first, self.up),
            (3, self.minus, self.second, self.down),
        ):
            self.copies[slot].wait_recv()

            def body(index):
                at = put(index, self.dims, self.axis, pos) + (self.rows, lanes)
                total = self.home[at] + self.got[(slot,) + index].astype(F32)
                self.out[at] = total.astype(self.out.dtype)

            each(self.rest, body)
            self.go(slot + 2, pos, lanes, dev)

    def finish(self, store):
        for slot in (1, 4, 2, 5):
            self.copies[slot].wait_recv()

        def body(index):
            for half, lanes, one, two in ((0, self.first, 2, 4), (1, self.second, 1, 5)):
                at = put(index, self.dims, self.axis, self.me) + (self.rows, lanes)
                total = self.home[at] + self.got[(one,) + index].astype(F32)
                store(index, half, total + self.got[(two,) + index].astype(F32))

        each(self.rest, body)
        for copy in self.copies.values():
            copy.wait_send()


class Gather:
    def __init__(self, place, wires, axis, ref, base, size, lanes, halves, mate=None):
        self.ref, self.base, self.size, self.mate = ref, base, size, mate
        self.lanes, self.halves = lanes, halves
        self.wires, self.first = wires, wires.take(8)
        me = position(axis, place)
        self.me, self.plus, self.minus, self.opposite = me, (me + 1) % 4, (me + 3) % 4, (me + 2) % 4
        self.up, self.down = along(axis, self.plus, place), along(axis, self.minus, place)
        self.copies = []
        self.passed = []

    def go(self, slot, pos, lanes, dev):
        rows = pl.ds(pl.multiple_of(self.base + pos * self.size, self.size), self.size)
        part = self.ref.at[rows, lanes]
        return self.wires.send(self.first + slot, part, part, dev)

    def share(self, slot, pos):
        if self.mate is not None:
            self.passed.append(self.go(slot, pos, self.lanes, self.mate))

    def begin(self):
        self.copies += [self.go(0, self.me, self.lanes, self.up)]
        self.copies += [self.go(1, self.me, self.lanes, self.down)]
        self.share(4, self.me)

    def relay(self):
        self.copies[0].wait_recv()
        self.copies += [self.go(2, self.minus, self.halves[0], self.up)]
        self.copies[1].wait_recv()
        self.copies += [self.go(3, self.plus, self.halves[1], self.down)]
        self.share(5, self.minus)
        self.share(6, self.plus)

    def arrive(self):
        self.copies[2].wait_recv()
        self.copies[3].wait_recv()
        self.share(7, self.opposite)

    def finish(self):
        for copy in self.passed:
            copy.wait_recv()
        for copy in self.copies + self.passed:
            copy.wait_send()


def row_of(block, k):
    return jnp.broadcast_to(block[k : k + 1, :], block.shape)


def pieces(value, count):
    terms = []
    for _ in range(count):
        term = value.astype(BF16).astype(F32)
        terms.append(term)
        value = value - term
    return terms


def eliminate(rows, right, cols, sub):
    scale = jnp.zeros((8, 128), F32)
    for k in range(8):
        inv = 1.0 / row_of(cols[0][k], k)
        scale = jnp.where(sub == k, inv, scale)
        pivot_row = row_of(rows[0], k)
        pivot_right = row_of(right[0], k)
        heads = [row_of(cols[0][m], k) for m in range(k + 1, 8)]
        for t in range(len(rows)):
            mult = cols[t][k] * inv
            if t == 0:
                mult = jnp.where(sub > k, mult, 0.0)
            for i, m in enumerate(range(k + 1, 8)):
                cols[t][m] = cols[t][m] - mult * heads[i]
            rows[t] = rows[t] - mult * pivot_row
            right[t] = right[t] - mult * pivot_right
    return rows, right, scale


def stack_dot(left, right):
    a1, a2, a3 = pieces(left, 3)
    b1, b2, b3 = pieces(right, 3)
    a = jnp.concatenate([a1, a1, a2, a2, a1, a3], axis=0).astype(BF16)
    b = jnp.concatenate([b1, b2, b1, b2, b3, b1], axis=0).astype(BF16)
    return lax.dot_general(a, b, (((0,), (0,)), ((), ())), preferred_element_type=F32)


def factor_block(a_ref, x_ref, middle):
    sub = lax.broadcasted_iota(jnp.int32, (8, 128), 0)
    row = lax.broadcasted_iota(jnp.int32, (128, 128), 0)
    lane = lax.broadcasted_iota(jnp.int32, (128, 128), 1)
    x_ref[...] = jnp.where(row == lane, 1.0, 0.0).astype(F32)
    for g in range(16):
        b = g * 8
        n = 2 if g < 15 else 1
        rows = [a_ref[b + 8 * t : b + 8 * t + 8, :] for t in range(n)]
        right = [x_ref[b + 8 * t : b + 8 * t + 8, :] for t in range(n)]
        cols = [
            [jnp.broadcast_to(rows[t][:, b + m : b + m + 1], (8, 128)) for m in range(8)]
            for t in range(n)
        ]
        rows, right, scale = eliminate(rows, right, cols, sub)
        if n == 2:
            a_ref[b + 8 : b + 16, :] = rows[1]
            x_ref[b + 8 : b + 16, :] = right[1]
        if g < 14:
            low = b + 16
            both = jnp.concatenate([rows[0], right[0]], axis=1)
            change = stack_dot(rows[0] * scale, both)
            a_ref[low:, :] = a_ref[low:, :] - change[low:, :128]
            x_ref[low:, :] = x_ref[low:, :] - change[low:, 128:]
        x_ref[b : b + 8, :] = right[0] * jnp.sqrt(scale)
        middle(g)


def two(value):
    high = value.astype(BF16)
    return high, (value - high.astype(F32)).astype(BF16)


def dot_two(left, right):
    lh, ll = two(left)
    rh, rl = two(right)
    return jnp.dot(
        jnp.concatenate([lh, ll, lh], axis=1),
        jnp.concatenate([rh, rh, rl], axis=0),
        preferred_element_type=F32,
    )


def invert_factor(work, a_ref, x_ref, between):
    n = work.shape[0]
    for k in range(n // 128):
        b, e = k * 128, k * 128 + 128
        a_ref[...] = work[b:e, b:e]
        factor_block(a_ref, x_ref, between)
        inverse = x_ref[...]
        for low, high in ((0, b), (e, n)):
            if low < high:
                work[b:e, low:high] = dot_two(inverse, work[b:e, low:high])
        work[b:e, b:e] = inverse
        if e < n:
            high, low = two(work[b:e, :])
            left = jnp.concatenate([high[:, e:], low[:, e:], high[:, e:]], axis=0)
            both = jnp.concatenate([high, high, low], axis=0)
            change = lax.dot_general(
                left, both, (((0,), (0,)), ((), ())), preferred_element_type=F32
            )
            if b:
                work[e:, :b] = work[e:, :b] - change[:, :b]
            work[e:, b:e] = -change[:, b:e]
            work[e:, e:] = work[e:, e:] - change[:, e:]
        between(16)


DIMS = "xzy"
ORDERS = ("xyz", "yzx", "zxy")
LEAD_ORDERS = ("xyz", "yzx")
PARTS = ((0, 96), (96, 80), (176, 80))
EVERY = slice(None)
CHUNKS = COLS // 128


def kernel(
    basis, cond, ground, tile, factor, other,
    panel, scaled, faces, halos, hz, image, image_t,
    lead_window, lead_home, lead_out, window, home, out, work, a_ref, x_ref, total, rows_t,
    *rest,
):
    lead_gots, lead_sums, gots, sums = rest[:6], rest[6:10], rest[10:19], rest[19:25]
    load_sem, send_sem, recv_sem = rest[25:]
    wires = Wires(send_sem, recv_sem)
    gx, gy, gz = lax.axis_index("gx"), lax.axis_index("gy"), lax.axis_index("gz")
    place = here()
    x, y, z, core = place
    mate = device(x, y, z, 1 - core)
    beside = [
        ((gx + 7) % 8, gy, gz),
        ((gx + 1) % 8, gy, gz),
        (gx, (gy + 7) % 8, gz),
        (gx, (gy + 1) % 8, gz),
        (gx, gy, 1 - gz),
    ]
    load = pltpu.make_async_copy(basis.at[:, pl.ds(0, COLS)], panel, load_sem.at[0])
    load.start()
    own_lead = []
    for rb in range(2):
        begin = pl.multiple_of(rb * 512 + core * 256, 256)
        own_lead.append(
            pltpu.make_async_copy(
                basis.at[:, pl.ds(begin, 256)],
                lead_window.at[pl.ds(0, 512), pl.ds(rb * 256, 256)],
                load_sem.at[1 + rb],
            )
        )
        own_lead[rb].start()
    greet(beside + torus_peers(place))

    swap_base = wires.take(16)

    def swap(rb, dst):
        begin = pl.multiple_of(rb * 512 + (1 - core) * 256, 256)
        return wires.copy(swap_base + rb, basis.at[:, pl.ds(begin, 256)], dst, mate)

    def far(rb):
        return other.at[:, pl.ds(pl.multiple_of(rb * 256, 256), 256)]

    lead_swaps = [
        swap(rb, lead_window.at[pl.ds(512, 512), pl.ds(rb * 256, 256)]) for rb in range(2)
    ]
    for copy in lead_swaps:
        copy.start()
    load.wait()

    def scale(c, _):
        lanes = pl.ds(pl.multiple_of(c * 128, 128), 128)
        inner = lax.broadcasted_iota(jnp.int32, (8, 128), 0)
        y_low, y_high, z_face = [], [], []
        for i in range(8):
            rows = pl.ds(i * 64, 64)
            value = (cond[rows, :] * panel[rows, lanes].astype(F32)).astype(BF16)
            scaled[rows, lanes] = value
            if i == 0:
                faces[0, :, lanes] = value
            if i == 7:
                faces[1, :, lanes] = value
            value = value.astype(F32)
            y_low.append(value[:8])
            y_high.append(value[56:])
            face = jnp.zeros((8, 128), F32)
            for j in range(8):
                cell = value[j * 8 : j * 8 + 8]
                low = jnp.broadcast_to(cell[0:1, :], (8, 128))
                high = jnp.broadcast_to(cell[7:8, :], (8, 128))
                face = jnp.where(inner == j, jnp.where(gz == 1, low, high), face)
            z_face.append(face)
        for f, face in ((2, y_low), (3, y_high), (4, z_face)):
            faces[f, :, lanes] = jnp.concatenate(face, axis=0).astype(BF16)
        return 0

    lax.fori_loop(0, CHUNKS, scale, 0)
    lands = [1, 0, 3, 2, 4]
    face_base = wires.take(5)
    face_copies = [
        wires.send(face_base + f, faces.at[f], halos.at[lands[f]], beside[f]) for f in range(5)
    ]

    def start_swap(rb, _):
        swap(rb, far(rb)).start()
        return 0

    lax.fori_loop(2, 16, start_swap, 0)
    for copy in face_copies:
        copy.wait()

    keep = [gx > 0, gx < 7, gy > 0, gy < 7]
    image_base = wires.take(CHUNKS)

    def image_copy(c):
        lanes = pl.ds(pl.multiple_of(c * 128, 128), 128)
        return wires.copy(
            image_base + c, image.at[pl.ds(0, 512), lanes], image.at[pl.ds(512, 512), lanes], mate
        )

    def stencil(c, _):
        lanes = pl.ds(pl.multiple_of(c * 128, 128), 128)
        inner = lax.broadcasted_iota(jnp.int32, (64, 128), 0) % 8

        def halo(f):
            return jnp.where(keep[f], halos[f, :, lanes].astype(F32), 0.0)

        hz[...] = halos[4, :, lanes].astype(F32)
        x_low, x_high, y_low, y_high = halo(0), halo(1), halo(2), halo(3)
        for i in range(8):
            rows = pl.ds(i * 64, 64)
            me = scaled[rows, lanes].astype(F32)
            down = scaled[pl.ds((i - 1) * 64, 64), lanes].astype(F32) if i > 0 else x_low
            up = scaled[pl.ds((i + 1) * 64, 64), lanes].astype(F32) if i < 7 else x_high
            around = up + down
            around = around + jnp.concatenate([me[8:], y_high[i * 8 : i * 8 + 8]], axis=0)
            around = around + jnp.concatenate([y_low[i * 8 : i * 8 + 8], me[:56]], axis=0)
            ends = jnp.concatenate(
                [jnp.broadcast_to(hz[i * 8 + j : i * 8 + j + 1, :], (8, 128)) for j in range(8)],
                axis=0,
            )
            high = pltpu.roll(me, 63, 0)
            low = pltpu.roll(me, 1, 0)
            high = jnp.where(inner == 7, jnp.where(gz == 0, ends, 0.0), high)
            low = jnp.where(inner == 0, jnp.where(gz == 1, ends, 0.0), low)
            around = around + high + low
            value = cond[rows, :] * (6.0 * me - around)
            value = value + ground[rows, :] * panel[rows, lanes].astype(F32)
            image[rows, lanes] = value.astype(BF16)
        image_copy(c).start()
        return 0

    lax.fori_loop(0, CHUNKS, stencil, 0)

    def turn(c, _):
        image_copy(c).wait()
        rows = pl.ds(pl.multiple_of(c * 128, 128), 128)
        image_t[rows, :] = image[:, rows].T
        return 0

    lax.fori_loop(0, CHUNKS, turn, 0)

    for copy in own_lead + lead_swaps:
        copy.wait()

    def lead_terms(c, _):
        rows = pl.ds(pl.multiple_of(c * 256, 256), 256)
        product = jnp.dot(image_t[rows, :], lead_window[...], preferred_element_type=F32)
        for i in range(16):
            value = product[i * 16 : i * 16 + 16, :]
            lead_home[c, i // 4, i % 4] = value
            lead_out[c, i // 4, i % 4] = value.astype(BF16)
        return 0

    lax.fori_loop(0, 4, lead_terms, 0)

    def fetch(rb):
        slot = rb % 2
        begin = pl.multiple_of(rb * 512 + core * 256, 256)
        return (
            pltpu.make_async_copy(
                basis.at[:, pl.ds(begin, 256)],
                window.at[slot, pl.ds(0, 512), :],
                load_sem.at[3 + slot],
            ),
            pltpu.make_async_copy(
                far(rb), window.at[slot, pl.ds(512, 512), :], load_sem.at[5 + slot]
            ),
        )

    def start_fetch(rb):
        swap(rb, far(rb)).wait()
        for copy in fetch(rb):
            copy.start()

    def multiply(rb, read):
        to_x, to_z = (rb % 2) * 2 + rb // 8, (rb // 2) % 4

        def one(c, _):
            rows = pl.ds(pl.multiple_of(c * 256, 256), 256)
            product = jnp.dot(image_t[rows, :], read(), preferred_element_type=F32)
            home[to_x, to_z, c] = product
            out[to_x, to_z, c] = product.astype(BF16)
            return 0

        lax.fori_loop(0, 4, one, 0)

    def terms(low, high):
        def one(rb, _):
            for copy in fetch(rb):
                copy.wait()

            @pl.when(rb < 15)
            def _():
                start_fetch(rb + 1)

            multiply(rb, lambda: window[rb % 2])
            return 0

        lax.fori_loop(low, high, one, 0)

    def lead_block(rb):
        multiply(rb, lambda: lead_window[:, rb * 256 : rb * 256 + 256])

    dims = [LEAD_ORDERS[p] for p in range(2)]
    homes, outs, lane = [lead_home] * 2, [lead_out] * 2, [0, 256]
    for stage in range(3):
        steps = [
            Reduce(
                place, wires, LEAD_ORDERS[p][stage], dims[p], homes[p], outs[p], EVERY, lane[p],
                lead_gots[p * 3 + stage],
            )
            for p in range(2)
        ]
        for step in steps:
            step.begin()
        for step in steps:
            step.follow()
        if stage == 0:
            start_fetch(2)
            lead_block(0)
            lead_block(1)
        else:
            terms(5 * stage, 5 * stage + 2)
        for step in steps:
            step.relay()
        if stage == 0:
            terms(2, 5)
        else:
            terms(5 * stage + 2, 5 * stage + 5)
        for p, step in enumerate(steps):
            if stage < 2:
                acc = lead_sums[p * 2 + stage]

                def store(index, half, value, acc=acc):
                    acc[index + (EVERY, pl.ds(half * 128, 128))] = value

                homes[p] = outs[p] = acc
                lane[p] = 0
            else:
                at = [position(axis, place) for axis in LEAD_ORDERS[p]]
                rows = pl.ds(pl.multiple_of((at[0] * 16 + at[1] * 4 + at[2]) * 16, 16), 16)

                def store(index, half, value, p=p, rows=rows):
                    begin = pl.multiple_of(p * 512 + core * 256 + half * 128, 128)
                    work[rows, pl.ds(begin, 128)] = value

            step.finish(store)
            dims[p] = step.rest
    def gather_rows():
        slots = [2 * ((y + d) % 4) + core for d in range(4)]
        up, down = along("y", (y + 1) % 4, place), along("y", (y + 3) % 4, place)
        base = wires.take(8)

        def go(number, slot, lanes, dev):
            block = rows_t.at[pl.ds(pl.multiple_of(slot * 128, 128), 128), lanes]
            return wires.send(base + number, block, block, dev)

        whole, low, high = pl.ds(0, 512), pl.ds(0, 256), pl.ds(256, 256)
        one, two = go(0, slots[0], whole, up), go(1, slots[0], whole, down)
        passed = [go(4, slots[0], whole, mate)]
        yield
        one.wait_recv()
        three = go(2, slots[3], low, up)
        passed += [go(5, slots[3], whole, mate)]
        two.wait_recv()
        four = go(3, slots[1], high, down)
        passed += [go(6, slots[1], whole, mate)]
        yield
        three.wait_recv()
        four.wait_recv()
        passed += [go(7, slots[2], whole, mate)]
        for copy in passed:
            copy.wait_recv()
        for copy in passed + [one, two, three, four]:
            copy.wait_send()

    def all_rows():
        dims, rows = [DIMS] * 3, [pl.ds(begin, size) for begin, size in PARTS]
        homes, outs = [home] * 3, [out] * 3
        for stage in range(3):
            steps = [
                Reduce(
                    place, wires, ORDERS[p][stage], dims[p], homes[p], outs[p], rows[p], 0,
                    gots[p * 3 + stage],
                )
                for p in range(3)
            ]
            for step in steps:
                step.begin()
            if stage == 0:
                yield
            for step in steps:
                step.follow()
            yield
            for step in steps:
                step.relay()
            yield
            for p, step in enumerate(steps):
                if stage < 2:
                    acc = sums[p * 2 + stage]

                    def store(index, half, value, acc=acc):
                        acc[index + (EVERY, pl.ds(half * 128, 128))] = value

                    homes[p] = outs[p] = acc
                    rows[p] = EVERY
                else:

                    def store(index, half, value, p=p):
                        total[pl.ds(*PARTS[p]), pl.ds(half * 128, 128)] = value

                step.finish(store)
                dims[p] = step.rest
        mine = pl.ds(pl.multiple_of(core * 128, 128), 128)
        theirs = pl.ds(pl.multiple_of((1 - core) * 128, 128), 128)
        lanes = pl.ds(pl.multiple_of(core * 256, 256), 256)
        swapped = wires.send(wires.take(), total.at[theirs, :], tile.at[:, lanes], mate)
        tile[:, lanes] = total[mine, :]
        yield
        swapped.wait()
        rows_t[pl.ds(pl.multiple_of(gy * 128, 128), 128), :] = tile[...]
        yield from gather_rows()

    events = all_rows()

    for stage in range(3):
        steps = []
        for p in range(2):
            at = [position(axis, place) for axis in LEAD_ORDERS[p]]
            base = (at[0] * 256 + at[1] * 64, at[0] * 256, 0)[stage]
            begin = pl.multiple_of(p * 512 + core * 256, 256)
            halves = [pl.ds(begin, 128), pl.ds(pl.multiple_of(begin + 128, 128), 128)]
            steps.append(
                Gather(
                    place, wires, LEAD_ORDERS[p][2 - stage], work, base, (16, 64, 256)[stage],
                    pl.ds(begin, 256), halves, mate if stage == 2 else None,
                )
            )
        for step in steps:
            step.begin()
        if stage == 0:
            terms(15, 16)
        for _ in range(AHEAD[2 * stage]):
            next(events)
        for step in steps:
            step.relay()
        for _ in range(AHEAD[2 * stage + 1]):
            next(events)
        if stage < 2:
            for step in steps:
                step.arrive()
                step.finish()

    for step in steps:
        step.arrive()
    for step in steps:
        step.finish()
    for b in range(0, COLS, NB):
        block = work[b : b + NB, b : b + NB]
        work[b : b + NB, b : b + NB] = 0.5 * (block + block.T)
    count = [0]

    def between(_):
        if count[0] in WHEN:
            next(events)
        count[0] += 1

    invert_factor(work, a_ref, x_ref, between)
    for _ in events:
        pass
    block = work[pl.ds(pl.multiple_of(gy * 128, 128), 128), :]
    lane = lax.broadcasted_iota(jnp.int32, block.shape, 1)
    block = jnp.where(lane < (gy + 1) * 128, block, 0.0)
    mine = dot_two(block, rows_t[...])
    column = gy * 128 + lax.broadcasted_iota(jnp.int32, mine.shape, 0)
    row = (gx * 2 + gz) * 512 + lax.broadcasted_iota(jnp.int32, mine.shape, 1)
    factor[...] = jnp.where(column <= row, mine, 0.0).T


AHEAD = (1, 0, 1, 0, 0, 1)
WHEN = (35, 55, 74, 98, 110, 126)
WIRES = 180


def project(basis, cond, ground):
    any_spec = pl.BlockSpec(memory_space=pltpu.HBM)
    vmem = pl.BlockSpec(memory_space=pltpu.VMEM)
    lead_gots, lead_sums, gots, sums = [], [], [], []
    for _ in range(2):
        lead_gots += [
            pltpu.VMEM((6, 4, 4, 16, 128), BF16),
            pltpu.VMEM((6, 4, 16, 128), F32),
            pltpu.VMEM((6, 16, 128), F32),
        ]
        lead_sums += [pltpu.VMEM((4, 4, 16, 256), F32), pltpu.VMEM((4, 16, 256), F32)]
    for _, size in PARTS:
        gots += [
            pltpu.VMEM((6, 4, 4, size, 128), BF16),
            pltpu.VMEM((6, 4, size, 128), F32),
            pltpu.VMEM((6, size, 128), F32),
        ]
        sums += [pltpu.VMEM((4, 4, size, 256), F32), pltpu.VMEM((4, size, 256), F32)]
    return pl.pallas_call(
        kernel,
        out_shape=(
            jax.ShapeDtypeStruct((128, 512), F32),
            jax.ShapeDtypeStruct((512, 128), F32),
            jax.ShapeDtypeStruct((512, 4096), BF16),
        ),
        in_specs=[any_spec, vmem, vmem],
        out_specs=(vmem, vmem, any_spec),
        scratch_shapes=[
            pltpu.VMEM((512, COLS), BF16),
            pltpu.VMEM((512, COLS), BF16),
            pltpu.VMEM((5, 64, COLS), BF16),
            pltpu.VMEM((5, 64, COLS), BF16),
            pltpu.VMEM((64, 128), F32),
            pltpu.VMEM((1024, COLS), BF16),
            pltpu.VMEM((COLS, 1024), BF16),
            pltpu.VMEM((1024, 512), BF16),
            pltpu.VMEM((4, 4, 4, 16, 512), F32),
            pltpu.VMEM((4, 4, 4, 16, 512), BF16),
            pltpu.VMEM((2, 1024, 256), BF16),
            pltpu.VMEM((4, 4, 4, 256, 256), F32),
            pltpu.VMEM((4, 4, 4, 256, 256), BF16),
            pltpu.VMEM((COLS, COLS), F32),
            pltpu.VMEM((128, 128), F32),
            pltpu.VMEM((128, 128), F32),
            pltpu.VMEM((256, 256), F32),
            pltpu.VMEM((COLS, 512), F32),
            *lead_gots,
            *lead_sums,
            *gots,
            *sums,
            pltpu.SemaphoreType.DMA((7,)),
            pltpu.SemaphoreType.DMA((WIRES,)),
            pltpu.SemaphoreType.DMA((WIRES,)),
        ],
        compiler_params=pltpu.CompilerParams(
            collective_id=0, has_side_effects=True, vmem_limit_bytes=67043328
        ),
        name="project",
    )(basis, cond, ground)


def local(basis, classes, cond_table, ground_table, port_cells, port_load):
    cells_x, cells_y, cells_z, width = basis.shape
    cells = cells_x * cells_y * cells_z
    place = [
        lax.axis_index(axis) * size + jnp.arange(size, dtype=jnp.int32)
        for axis, size in (("gx", cells_x), ("gy", cells_y), ("gz", cells_z))
    ]
    total_y, total_z = cells_y * lax.axis_size("gy"), cells_z * lax.axis_size("gz")
    flat_ids = (
        (place[0][:, None, None] * total_y + place[1][None, :, None]) * total_z
        + place[2][None, None, :]
    ).reshape(cells)
    flat_classes = classes.reshape(cells)
    onehot = (flat_classes[:, None] == jnp.arange(16, dtype=jnp.int32)).astype(F32)
    conduct = jnp.sum(onehot * cond_table, axis=1)
    grounds = jnp.sum(onehot * ground_table, axis=1)
    matches = flat_ids[:, None] == port_cells[None, :]
    grounds = grounds + jnp.sum(jnp.where(matches, port_load[None, :], 0.0), axis=1)
    cond = jnp.broadcast_to(conduct[:, None], (cells, 128))
    ground = jnp.broadcast_to(grounds[:, None], (cells, 128))
    flat = basis.reshape(cells, width)
    tile, factor, _ = project(flat, cond, ground)
    return tile.T, factor


def solution(mesh):
    placed = (P("gx", "gy", "gz", None), P("gx", "gy", "gz"), P(), P(), P(), P())
    return jax.shard_map(
        local,
        mesh=mesh,
        in_specs=placed,
        out_specs=(P(("gx", "gz"), "gy"), P(("gx", "gz"), "gy")),
        check_vma=False,
    )
```

```python
import jax
import jax.numpy as jnp
from jax import lax
from jax.experimental import pallas as pl
from jax.experimental.pallas import tpu as pltpu
from jax.sharding import PartitionSpec as P

NB = 512
PANELS = 2
COLS = NB * PANELS
F32 = jnp.float32
BF16 = jnp.bfloat16
MESH = pl.DeviceIdType.MESH


def here():
    gx, gy, gz = lax.axis_index("gx"), lax.axis_index("gy"), lax.axis_index("gz")
    return gz * 2 + gx // 4, gy // 2, gx % 4, gy % 2


def device(x, y, z, core):
    return ((x % 2) * 4 + z, y * 2 + core, x // 2)


def along(axis, pos, place):
    x, y, z, core = place
    if axis == "x":
        x = pos
    elif axis == "y":
        y = pos
    else:
        z = pos
    return device(x, y, z, core)


def position(axis, place):
    return place["xyz".index(axis)]


def greet(devices):
    barrier = pltpu.get_barrier_semaphore()
    for dev in devices:
        pl.semaphore_signal(barrier, inc=1, device_id=dev, device_id_type=MESH)
    pl.semaphore_wait(barrier, len(devices))


def torus_peers(place):
    x, y, z, core = place
    peers = []
    for axis in "xyz":
        pos = position(axis, place)
        peers += [along(axis, (pos + 1) % 4, place), along(axis, (pos + 3) % 4, place)]
    return peers + [device(x, y, z, 1 - core)]


class Wires:
    def __init__(self, send_sem, recv_sem):
        self.send_sem, self.recv_sem, self.used = send_sem, recv_sem, 0

    def take(self, count=1):
        self.used += count
        return self.used - count

    def copy(self, number, src, dst, dev):
        return pltpu.make_async_remote_copy(
            src_ref=src,
            dst_ref=dst,
            send_sem=self.send_sem.at[number],
            recv_sem=self.recv_sem.at[number],
            device_id=dev,
            device_id_type=MESH,
        )

    def send(self, number, src, dst, dev):
        copy = self.copy(number, src, dst, dev)
        copy.start()
        return copy


def each(dims, body):
    count = 4 ** len(dims)
    if count == 1:
        body(())
        return

    def step(i, _):
        body(tuple((i // 4 ** (len(dims) - 1 - d)) % 4 for d in range(len(dims))))
        return 0

    lax.fori_loop(0, count, step, 0)


def put(index, dims, axis, pos):
    index = list(index)
    index.insert(dims.index(axis), pos)
    return tuple(index)


class Reduce:
    def __init__(self, place, wires, axis, dims, home, out, rows, lane, got):
        self.axis, self.dims, self.home, self.out, self.rows, self.got = axis, dims, home, out, rows, got
        self.first, self.second = pl.ds(lane, 128), pl.ds(lane + 128, 128)
        self.rest = tuple(d for d in dims if d != axis)
        self.wires, self.base = wires, wires.take(6)
        me = position(axis, place)
        self.me, self.plus, self.minus, self.opposite = me, (me + 1) % 4, (me + 3) % 4, (me + 2) % 4
        self.up, self.down = along(axis, self.plus, place), along(axis, self.minus, place)
        self.copies = {}

    def go(self, slot, pos, lanes, dev):
        index = put([pl.ds(0, 4)] * len(self.rest), self.dims, self.axis, pos)
        src = self.out.at[index + (self.rows, lanes)]
        self.copies[slot] = self.wires.send(self.base + slot, src, self.got.at[slot], dev)

    def begin(self):
        self.go(0, self.opposite, self.first, self.up)
        self.go(3, self.opposite, self.second, self.down)

    def follow(self):
        self.go(1, self.plus, self.second, self.up)
        self.go(4, self.minus, self.first, self.down)

    def relay(self):
        for slot, pos, lanes, dev in (
            (0, self.plus, self.first, self.up),
            (3, self.minus, self.second, self.down),
        ):
            self.copies[slot].wait_recv()

            def body(index):
                at = put(index, self.dims, self.axis, pos) + (self.rows, lanes)
                total = self.home[at] + self.got[(slot,) + index].astype(F32)
                self.out[at] = total.astype(self.out.dtype)

            each(self.rest, body)
            self.go(slot + 2, pos, lanes, dev)

    def finish(self, store):
        for slot in (1, 4, 2, 5):
            self.copies[slot].wait_recv()

        def body(index):
            for half, lanes, one, two in ((0, self.first, 2, 4), (1, self.second, 1, 5)):
                at = put(index, self.dims, self.axis, self.me) + (self.rows, lanes)
                total = self.home[at] + self.got[(one,) + index].astype(F32)
                store(index, half, total + self.got[(two,) + index].astype(F32))

        each(self.rest, body)
        for copy in self.copies.values():
            copy.wait_send()


class Gather:
    def __init__(self, place, wires, axis, ref, base, size, lanes, halves, mate=None):
        self.ref, self.base, self.size, self.mate = ref, base, size, mate
        self.lanes, self.halves = lanes, halves
        self.wires, self.first = wires, wires.take(10)
        me = position(axis, place)
        self.me, self.plus, self.minus, self.opposite = me, (me + 1) % 4, (me + 3) % 4, (me + 2) % 4
        self.up, self.down = along(axis, self.plus, place), along(axis, self.minus, place)
        self.copies = []
        self.passed = []

    def go(self, slot, pos, lanes, dev):
        rows = pl.ds(pl.multiple_of(self.base + pos * self.size, self.size), self.size)
        part = self.ref.at[rows, lanes]
        return self.wires.send(self.first + slot, part, part, dev)

    def share(self, slot, pos):
        if self.mate is not None:
            self.passed.append(self.go(slot, pos, self.lanes, self.mate))

    def begin(self):
        low, high = self.halves
        self.copies += [self.go(0, self.me, low, self.up), self.go(1, self.me, high, self.down)]
        self.copies += [self.go(8, self.me, high, self.up), self.go(9, self.me, low, self.down)]
        self.share(4, self.me)

    def relay(self):
        low, high = self.halves
        self.copies[0].wait_recv()
        self.copies += [self.go(2, self.minus, low, self.up)]
        self.copies[1].wait_recv()
        self.copies += [self.go(3, self.plus, high, self.down)]

    def pass_on(self):
        self.copies[2].wait_recv()
        self.copies[3].wait_recv()
        self.share(5, self.minus)
        self.share(6, self.plus)

    def arrive(self):
        self.copies[4].wait_recv()
        self.copies[5].wait_recv()
        self.share(7, self.opposite)

    def finish(self):
        for copy in self.passed:
            copy.wait_recv()
        for copy in self.copies + self.passed:
            copy.wait_send()


def row_of(block, k):
    return jnp.broadcast_to(block[k : k + 1, :], block.shape)


def pieces(value, count):
    terms = []
    for _ in range(count):
        term = value.astype(BF16).astype(F32)
        terms.append(term)
        value = value - term
    return terms


def eliminate(rows, right, cols, sub):
    scale = jnp.zeros((8, 128), F32)
    for k in range(8):
        inv = 1.0 / row_of(cols[0][k], k)
        scale = jnp.where(sub == k, inv, scale)
        pivot_row = row_of(rows[0], k)
        pivot_right = row_of(right[0], k)
        heads = [row_of(cols[0][m], k) for m in range(k + 1, 8)]
        for t in range(len(rows)):
            mult = cols[t][k] * inv
            if t == 0:
                mult = jnp.where(sub > k, mult, 0.0)
            for i, m in enumerate(range(k + 1, 8)):
                cols[t][m] = cols[t][m] - mult * heads[i]
            rows[t] = rows[t] - mult * pivot_row
            right[t] = right[t] - mult * pivot_right
    return rows, right, scale


def stack_dot(left, right):
    a1, a2, a3 = pieces(left, 3)
    b1, b2, b3 = pieces(right, 3)
    a = jnp.concatenate([a1, a1, a2, a2, a1, a3], axis=0).astype(BF16)
    b = jnp.concatenate([b1, b2, b1, b2, b3, b1], axis=0).astype(BF16)
    return lax.dot_general(a, b, (((0,), (0,)), ((), ())), preferred_element_type=F32)


def factor_block(a_ref, x_ref, middle):
    sub = lax.broadcasted_iota(jnp.int32, (8, 128), 0)
    row = lax.broadcasted_iota(jnp.int32, (128, 128), 0)
    lane = lax.broadcasted_iota(jnp.int32, (128, 128), 1)
    x_ref[...] = jnp.where(row == lane, 1.0, 0.0).astype(F32)
    for g in range(16):
        b = g * 8
        n = 2 if g < 15 else 1
        rows = [a_ref[b + 8 * t : b + 8 * t + 8, :] for t in range(n)]
        right = [x_ref[b + 8 * t : b + 8 * t + 8, :] for t in range(n)]
        cols = [
            [jnp.broadcast_to(rows[t][:, b + m : b + m + 1], (8, 128)) for m in range(8)]
            for t in range(n)
        ]
        rows, right, scale = eliminate(rows, right, cols, sub)
        if n == 2:
            a_ref[b + 8 : b + 16, :] = rows[1]
            x_ref[b + 8 : b + 16, :] = right[1]
        if g < 14:
            low = b + 16
            both = jnp.concatenate([rows[0], right[0]], axis=1)
            change = stack_dot(rows[0] * scale, both)
            a_ref[low:, :] = a_ref[low:, :] - change[low:, :128]
            x_ref[low:, :] = x_ref[low:, :] - change[low:, 128:]
        x_ref[b : b + 8, :] = right[0] * jnp.sqrt(scale)
        middle(g)


def two(value):
    high = value.astype(BF16)
    return high, (value - high.astype(F32)).astype(BF16)


def dot_two(left, right):
    lh, ll = two(left)
    rh, rl = two(right)
    return jnp.dot(
        jnp.concatenate([lh, ll, lh], axis=1),
        jnp.concatenate([rh, rh, rl], axis=0),
        preferred_element_type=F32,
    )


def invert_factor(work, a_ref, x_ref, between):
    n = work.shape[0]
    for k in range(n // 128):
        b, e = k * 128, k * 128 + 128
        a_ref[...] = work[b:e, b:e]
        factor_block(a_ref, x_ref, between)
        inverse = x_ref[...]
        for low, high in ((0, b), (e, n)):
            if low < high:
                work[b:e, low:high] = dot_two(inverse, work[b:e, low:high])
        work[b:e, b:e] = inverse
        if e < n:
            high, low = two(work[b:e, :])
            left = jnp.concatenate([high[:, e:], low[:, e:], high[:, e:]], axis=0)
            both = jnp.concatenate([high, high, low], axis=0)
            change = lax.dot_general(
                left, both, (((0,), (0,)), ((), ())), preferred_element_type=F32
            )
            if b:
                work[e:, :b] = work[e:, :b] - change[:, :b]
            work[e:, b:e] = -change[:, b:e]
            work[e:, e:] = work[e:, e:] - change[:, e:]
        between(16)


DIMS = "xzy"
ORDERS = ("xyz", "yzx", "zxy")
LEAD_ORDERS = ("xyz", "yzx")
PARTS = ((0, 96), (96, 80), (176, 80))
EVERY = slice(None)
CHUNKS = COLS // 128


def kernel(
    basis, classes, cond_table, ground_table, port_cells, port_load, tile, factor, other,
    cond, ground, panel, scaled, faces, halos, hz, image, image_t,
    lead_window, lead_home, lead_out, window, home, out, work, a_ref, x_ref, total, rows_t,
    *rest,
):
    lead_gots, lead_sums, gots, sums = rest[:6], rest[6:10], rest[10:19], rest[19:25]
    load_sem, send_sem, recv_sem = rest[25:]
    wires = Wires(send_sem, recv_sem)
    gx, gy, gz = lax.axis_index("gx"), lax.axis_index("gy"), lax.axis_index("gz")
    place = here()
    x, y, z, core = place
    mate = device(x, y, z, 1 - core)
    beside = [
        ((gx + 7) % 8, gy, gz),
        ((gx + 1) % 8, gy, gz),
        (gx, (gy + 7) % 8, gz),
        (gx, (gy + 1) % 8, gz),
        (gx, gy, 1 - gz),
    ]
    load = pltpu.make_async_copy(basis.at[:, pl.ds(0, COLS)], panel, load_sem.at[0])
    load.start()
    own_lead = []
    for rb in range(2):
        begin = pl.multiple_of(rb * 512 + core * 256, 256)
        own_lead.append(
            pltpu.make_async_copy(
                basis.at[:, pl.ds(begin, 256)],
                lead_window.at[pl.ds(0, 512), pl.ds(rb * 256, 256)],
                load_sem.at[1 + rb],
            )
        )
        own_lead[rb].start()
    greet(beside + torus_peers(place))

    swap_base = wires.take(16)

    def swap(rb, dst):
        begin = pl.multiple_of(rb * 512 + (1 - core) * 256, 256)
        return wires.copy(swap_base + rb, basis.at[:, pl.ds(begin, 256)], dst, mate)

    def far(rb):
        return other.at[:, pl.ds(pl.multiple_of(rb * 256, 256), 256)]

    lead_swaps = [
        swap(rb, lead_window.at[pl.ds(512, 512), pl.ds(rb * 256, 256)]) for rb in range(2)
    ]
    for copy in lead_swaps:
        copy.start()

    def look_up(i, _):
        kinds = classes[i]
        lane = lax.broadcasted_iota(jnp.int32, (8, 8), 1)
        diagonal = lane == lax.broadcasted_iota(jnp.int32, (8, 8), 0)
        for table, out_ref in ((cond_table, cond), (ground_table, ground)):
            values = jnp.zeros((8, 8), F32)
            for kind in range(16):
                values = jnp.where(kinds == kind, table[kind], values)
            columns = []
            for j in range(8):
                line = jnp.broadcast_to(values[j : j + 1, :], (8, 8))
                line = jnp.sum(jnp.where(diagonal, line, 0.0), axis=1, keepdims=True)
                columns.append(jnp.broadcast_to(line, (8, 128)))
            rows = pl.ds(pl.multiple_of(i * 64, 64), 64)
            out_ref[rows, :] = jnp.concatenate(columns, axis=0)
        return 0

    lax.fori_loop(0, 8, look_up, 0)
    load.wait()

    def scale(c, _):
        lanes = pl.ds(pl.multiple_of(c * 128, 128), 128)
        inner = lax.broadcasted_iota(jnp.int32, (8, 128), 0)
        y_low, y_high, z_face = [], [], []
        for i in range(8):
            rows = pl.ds(i * 64, 64)
            value = (cond[rows, :] * panel[rows, lanes].astype(F32)).astype(BF16)
            scaled[rows, lanes] = value
            if i == 0:
                faces[0, :, lanes] = value
            if i == 7:
                faces[1, :, lanes] = value
            value = value.astype(F32)
            y_low.append(value[:8])
            y_high.append(value[56:])
            face = jnp.zeros((8, 128), F32)
            for j in range(8):
                cell = value[j * 8 : j * 8 + 8]
                low = jnp.broadcast_to(cell[0:1, :], (8, 128))
                high = jnp.broadcast_to(cell[7:8, :], (8, 128))
                face = jnp.where(inner == j, jnp.where(gz == 1, low, high), face)
            z_face.append(face)
        for f, face in ((2, y_low), (3, y_high), (4, z_face)):
            faces[f, :, lanes] = jnp.concatenate(face, axis=0).astype(BF16)
        return 0

    lax.fori_loop(0, CHUNKS, scale, 0)
    lands = [1, 0, 3, 2, 4]
    face_base = wires.take(5)
    face_copies = [
        wires.send(face_base + f, faces.at[f], halos.at[lands[f]], beside[f]) for f in range(5)
    ]

    def start_swap(rb, _):
        swap(rb, far(rb)).start()
        return 0

    lax.fori_loop(2, 16, start_swap, 0)
    def add_ports(i, _):
        row = lax.broadcasted_iota(jnp.int32, (64, 128), 0)
        flat = ((gx * 8 + i) * 64 + gy * 8 + row // 8) * 16 + gz * 8 + row % 8
        found = jnp.zeros((64, 128), F32)
        for j in range(16):
            match = flat == jnp.broadcast_to(port_cells[j : j + 1, :], (64, 128))
            found = found + jnp.where(match, jnp.broadcast_to(port_load[j : j + 1, :], (64, 128)), 0.0)
        rows = pl.ds(pl.multiple_of(i * 64, 64), 64)
        ground[rows, :] = ground[rows, :] + jnp.sum(found, axis=1, keepdims=True)
        return 0

    lax.fori_loop(0, 8, add_ports, 0)
    for copy in face_copies:
        copy.wait()

    keep = [gx > 0, gx < 7, gy > 0, gy < 7]
    image_base = wires.take(CHUNKS)

    def image_copy(c):
        lanes = pl.ds(pl.multiple_of(c * 128, 128), 128)
        return wires.copy(
            image_base + c, image.at[pl.ds(0, 512), lanes], image.at[pl.ds(512, 512), lanes], mate
        )

    def stencil(c, _):
        lanes = pl.ds(pl.multiple_of(c * 128, 128), 128)
        inner = lax.broadcasted_iota(jnp.int32, (64, 128), 0) % 8

        def halo(f):
            return jnp.where(keep[f], halos[f, :, lanes].astype(F32), 0.0)

        hz[...] = halos[4, :, lanes].astype(F32)
        x_low, x_high, y_low, y_high = halo(0), halo(1), halo(2), halo(3)
        for i in range(8):
            rows = pl.ds(i * 64, 64)
            me = scaled[rows, lanes].astype(F32)
            down = scaled[pl.ds((i - 1) * 64, 64), lanes].astype(F32) if i > 0 else x_low
            up = scaled[pl.ds((i + 1) * 64, 64), lanes].astype(F32) if i < 7 else x_high
            around = up + down
            around = around + jnp.concatenate([me[8:], y_high[i * 8 : i * 8 + 8]], axis=0)
            around = around + jnp.concatenate([y_low[i * 8 : i * 8 + 8], me[:56]], axis=0)
            ends = jnp.concatenate(
                [jnp.broadcast_to(hz[i * 8 + j : i * 8 + j + 1, :], (8, 128)) for j in range(8)],
                axis=0,
            )
            high = pltpu.roll(me, 63, 0)
            low = pltpu.roll(me, 1, 0)
            high = jnp.where(inner == 7, jnp.where(gz == 0, ends, 0.0), high)
            low = jnp.where(inner == 0, jnp.where(gz == 1, ends, 0.0), low)
            around = around + high + low
            value = cond[rows, :] * (6.0 * me - around)
            value = value + ground[rows, :] * panel[rows, lanes].astype(F32)
            image[rows, lanes] = value.astype(BF16)
        image_copy(c).start()
        return 0

    lax.fori_loop(0, CHUNKS, stencil, 0)

    def turn(c, _):
        image_copy(c).wait()
        rows = pl.ds(pl.multiple_of(c * 128, 128), 128)
        image_t[rows, :] = image[:, rows].T
        return 0

    lax.fori_loop(0, CHUNKS, turn, 0)

    for copy in own_lead + lead_swaps:
        copy.wait()

    def lead_terms(c, _):
        rows = pl.ds(pl.multiple_of(c * 256, 256), 256)
        product = jnp.dot(image_t[rows, :], lead_window[...], preferred_element_type=F32)
        for i in range(16):
            value = product[i * 16 : i * 16 + 16, :]
            lead_home[c, i // 4, i % 4] = value
            lead_out[c, i // 4, i % 4] = value.astype(BF16)
        return 0

    lax.fori_loop(0, 4, lead_terms, 0)

    def fetch(rb):
        slot = rb % 2
        begin = pl.multiple_of(rb * 512 + core * 256, 256)
        return (
            pltpu.make_async_copy(
                basis.at[:, pl.ds(begin, 256)],
                window.at[slot, pl.ds(0, 512), :],
                load_sem.at[3 + slot],
            ),
            pltpu.make_async_copy(
                far(rb), window.at[slot, pl.ds(512, 512), :], load_sem.at[5 + slot]
            ),
        )

    def start_fetch(rb):
        swap(rb, far(rb)).wait()
        for copy in fetch(rb):
            copy.start()

    def multiply(rb, read):
        to_x, to_z = (rb % 2) * 2 + rb // 8, (rb // 2) % 4

        def one(c, _):
            rows = pl.ds(pl.multiple_of(c * 256, 256), 256)
            product = jnp.dot(image_t[rows, :], read(), preferred_element_type=F32)
            home[to_x, to_z, c] = product
            out[to_x, to_z, c] = product.astype(BF16)
            return 0

        lax.fori_loop(0, 4, one, 0)

    def terms(low, high):
        def one(rb, _):
            for copy in fetch(rb):
                copy.wait()

            @pl.when(rb < 15)
            def _():
                start_fetch(rb + 1)

            multiply(rb, lambda: window[rb % 2])
            return 0

        lax.fori_loop(low, high, one, 0)

    def lead_block(rb):
        multiply(rb, lambda: lead_window[:, rb * 256 : rb * 256 + 256])

    dims = [LEAD_ORDERS[p] for p in range(2)]
    homes, outs, lane = [lead_home] * 2, [lead_out] * 2, [0, 256]
    for stage in range(3):
        steps = [
            Reduce(
                place, wires, LEAD_ORDERS[p][stage], dims[p], homes[p], outs[p], EVERY, lane[p],
                lead_gots[p * 3 + stage],
            )
            for p in range(2)
        ]
        for step in steps:
            step.begin()
        for step in steps:
            step.follow()
        if stage == 0:
            start_fetch(2)
            lead_block(0)
            lead_block(1)
        else:
            terms(5 * stage, 5 * stage + 2)
        for step in steps:
            step.relay()
        if stage == 0:
            terms(2, 5)
        else:
            terms(5 * stage + 2, 5 * stage + 5)
        for p, step in enumerate(steps):
            if stage < 2:
                acc = lead_sums[p * 2 + stage]

                def store(index, half, value, acc=acc):
                    acc[index + (EVERY, pl.ds(half * 128, 128))] = value

                homes[p] = outs[p] = acc
                lane[p] = 0
            else:
                at = [position(axis, place) for axis in LEAD_ORDERS[p]]
                rows = pl.ds(pl.multiple_of((at[0] * 16 + at[1] * 4 + at[2]) * 16, 16), 16)

                def store(index, half, value, p=p, rows=rows):
                    begin = pl.multiple_of(p * 512 + core * 256 + half * 128, 128)
                    work[rows, pl.ds(begin, 128)] = value

            step.finish(store)
            dims[p] = step.rest
    def gather_rows():
        slots = [2 * ((y + d) % 4) + core for d in range(4)]
        up, down = along("y", (y + 1) % 4, place), along("y", (y + 3) % 4, place)
        base = wires.take(10)

        def go(number, slot, lanes, dev):
            block = rows_t.at[pl.ds(pl.multiple_of(slot * 128, 128), 128), lanes]
            return wires.send(base + number, block, block, dev)

        whole, low, high = pl.ds(0, 512), pl.ds(0, 256), pl.ds(256, 256)
        one, two = go(0, slots[0], low, up), go(1, slots[0], high, down)
        three, four = go(8, slots[0], high, up), go(9, slots[0], low, down)
        passed = [go(4, slots[0], whole, mate)]
        yield
        one.wait_recv()
        five = go(2, slots[3], low, up)
        two.wait_recv()
        six = go(3, slots[1], high, down)
        yield
        three.wait_recv()
        passed += [go(5, slots[3], whole, mate)]
        four.wait_recv()
        passed += [go(6, slots[1], whole, mate)]
        five.wait_recv()
        six.wait_recv()
        passed += [go(7, slots[2], whole, mate)]
        for copy in passed:
            copy.wait_recv()
        for copy in passed + [one, two, three, four, five, six]:
            copy.wait_send()

    def all_rows():
        dims, rows = [DIMS] * 3, [pl.ds(begin, size) for begin, size in PARTS]
        homes, outs = [home] * 3, [out] * 3
        for stage in range(3):
            steps = [
                Reduce(
                    place, wires, ORDERS[p][stage], dims[p], homes[p], outs[p], rows[p], 0,
                    gots[p * 3 + stage],
                )
                for p in range(3)
            ]
            for step in steps:
                step.begin()
            if stage == 0:
                yield
            for step in steps:
                step.follow()
            yield
            for step in steps:
                step.relay()
            yield
            for p, step in enumerate(steps):
                if stage < 2:
                    acc = sums[p * 2 + stage]

                    def store(index, half, value, acc=acc):
                        acc[index + (EVERY, pl.ds(half * 128, 128))] = value

                    homes[p] = outs[p] = acc
                    rows[p] = EVERY
                else:

                    def store(index, half, value, p=p):
                        total[pl.ds(*PARTS[p]), pl.ds(half * 128, 128)] = value

                step.finish(store)
                dims[p] = step.rest
        mine = pl.ds(pl.multiple_of(core * 128, 128), 128)
        theirs = pl.ds(pl.multiple_of((1 - core) * 128, 128), 128)
        lanes = pl.ds(pl.multiple_of(core * 256, 256), 256)
        swapped = wires.send(wires.take(), total.at[theirs, :], tile.at[:, lanes], mate)
        tile[:, lanes] = total[mine, :]
        yield
        swapped.wait()
        rows_t[pl.ds(pl.multiple_of(gy * 128, 128), 128), :] = tile[...]
        yield from gather_rows()

    events = all_rows()

    for stage in range(3):
        steps = []
        for p in range(2):
            at = [position(axis, place) for axis in LEAD_ORDERS[p]]
            base = (at[0] * 256 + at[1] * 64, at[0] * 256, 0)[stage]
            begin = pl.multiple_of(p * 512 + core * 256, 256)
            halves = [pl.ds(begin, 128), pl.ds(pl.multiple_of(begin + 128, 128), 128)]
            steps.append(
                Gather(
                    place, wires, LEAD_ORDERS[p][2 - stage], work, base, (16, 64, 256)[stage],
                    pl.ds(begin, 256), halves, mate if stage == 2 else None,
                )
            )
        for step in steps:
            step.begin()
        if stage == 0:
            terms(15, 16)
        for _ in range(AHEAD[2 * stage]):
            next(events)
        for step in steps:
            step.relay()
        for step in steps:
            step.pass_on()
        for _ in range(AHEAD[2 * stage + 1]):
            next(events)
        if stage < 2:
            for step in steps:
                step.arrive()
                step.finish()

    for step in steps:
        step.arrive()
    for step in steps:
        step.finish()
    for b in range(0, COLS, NB):
        block = work[b : b + NB, b : b + NB]
        work[b : b + NB, b : b + NB] = 0.5 * (block + block.T)
    count = [0]

    def between(_):
        if count[0] in WHEN:
            next(events)
        count[0] += 1

    invert_factor(work, a_ref, x_ref, between)
    for _ in events:
        pass
    block = work[pl.ds(pl.multiple_of(gy * 128, 128), 128), :]
    lane = lax.broadcasted_iota(jnp.int32, block.shape, 1)
    block = jnp.where(lane < (gy + 1) * 128, block, 0.0)
    mine = dot_two(block, rows_t[...])
    column = gy * 128 + lax.broadcasted_iota(jnp.int32, mine.shape, 0)
    row = (gx * 2 + gz) * 512 + lax.broadcasted_iota(jnp.int32, mine.shape, 1)
    factor[...] = jnp.where(column <= row, mine, 0.0)


AHEAD = (1, 0, 1, 0, 0, 1)
WHEN = (35, 55, 80, 94, 104, 111, 128)
WIRES = 200


def project(basis, classes, cond_table, ground_table, port_cells, port_load):
    any_spec = pl.BlockSpec(memory_space=pltpu.HBM)
    vmem = pl.BlockSpec(memory_space=pltpu.VMEM)
    smem = pl.BlockSpec(memory_space=pltpu.SMEM)
    lead_gots, lead_sums, gots, sums = [], [], [], []
    for _ in range(2):
        lead_gots += [
            pltpu.VMEM((6, 4, 4, 16, 128), BF16),
            pltpu.VMEM((6, 4, 16, 128), F32),
            pltpu.VMEM((6, 16, 128), F32),
        ]
        lead_sums += [pltpu.VMEM((4, 4, 16, 256), F32), pltpu.VMEM((4, 16, 256), F32)]
    for _, size in PARTS:
        gots += [
            pltpu.VMEM((6, 4, 4, size, 128), BF16),
            pltpu.VMEM((6, 4, size, 128), F32),
            pltpu.VMEM((6, size, 128), F32),
        ]
        sums += [pltpu.VMEM((4, 4, size, 256), F32), pltpu.VMEM((4, size, 256), F32)]
    return pl.pallas_call(
        kernel,
        out_shape=(
            jax.ShapeDtypeStruct((128, 512), F32),
            jax.ShapeDtypeStruct((128, 512), F32),
            jax.ShapeDtypeStruct((512, 4096), BF16),
        ),
        in_specs=[any_spec, vmem, smem, smem, vmem, vmem],
        out_specs=(vmem, vmem, any_spec),
        scratch_shapes=[
            pltpu.VMEM((512, 128), F32),
            pltpu.VMEM((512, 128), F32),
            pltpu.VMEM((512, COLS), BF16),
            pltpu.VMEM((512, COLS), BF16),
            pltpu.VMEM((5, 64, COLS), BF16),
            pltpu.VMEM((5, 64, COLS), BF16),
            pltpu.VMEM((64, 128), F32),
            pltpu.VMEM((1024, COLS), BF16),
            pltpu.VMEM((COLS, 1024), BF16),
            pltpu.VMEM((1024, 512), BF16),
            pltpu.VMEM((4, 4, 4, 16, 512), F32),
            pltpu.VMEM((4, 4, 4, 16, 512), BF16),
            pltpu.VMEM((2, 1024, 256), BF16),
            pltpu.VMEM((4, 4, 4, 256, 256), F32),
            pltpu.VMEM((4, 4, 4, 256, 256), BF16),
            pltpu.VMEM((COLS, COLS), F32),
            pltpu.VMEM((128, 128), F32),
            pltpu.VMEM((128, 128), F32),
            pltpu.VMEM((256, 256), F32),
            pltpu.VMEM((COLS, 512), F32),
            *lead_gots,
            *lead_sums,
            *gots,
            *sums,
            pltpu.SemaphoreType.DMA((7,)),
            pltpu.SemaphoreType.DMA((WIRES,)),
            pltpu.SemaphoreType.DMA((WIRES,)),
        ],
        compiler_params=pltpu.CompilerParams(
            collective_id=0, has_side_effects=True, vmem_limit_bytes=67043328
        ),
        name="project",
    )(basis, classes, cond_table, ground_table, port_cells, port_load)


def turn_kernel(tile, factor, tile_out, factor_out):
    tile_out[...] = tile[...].T
    factor_out[...] = factor[...].T


def local(basis, classes, cond_table, ground_table, port_cells, port_load):
    flat = basis.reshape(512, basis.shape[3])
    tile, factor, _ = project(
        flat, classes, cond_table, ground_table, port_cells.reshape(16, 128), port_load.reshape(16, 128)
    )
    shape = jax.ShapeDtypeStruct((512, 128), F32)
    return pl.pallas_call(turn_kernel, out_shape=(shape, shape), name="turn")(tile, factor)


def solution(mesh):
    placed = (P("gx", "gy", "gz", None), P("gx", "gy", "gz"), P(), P(), P(), P())
    return jax.shard_map(
        local,
        mesh=mesh,
        in_specs=placed,
        out_specs=(P(("gx", "gz"), "gy"), P(("gx", "gz"), "gy")),
        check_vma=False,
    )
```

```python
import jax
import jax.numpy as jnp
from jax import lax
from jax.experimental import pallas as pl
from jax.experimental.pallas import tpu as pltpu
from jax.sharding import PartitionSpec as P

NB = 512
PANELS = 2
COLS = NB * PANELS
F32 = jnp.float32
BF16 = jnp.bfloat16
MESH = pl.DeviceIdType.MESH
EVERY = slice(None)


def here():
    gx, gy, gz = lax.axis_index("gx"), lax.axis_index("gy"), lax.axis_index("gz")
    return gz * 2 + gx // 4, gy // 2, gx % 4, gy % 2


def device(x, y, z, core):
    return ((x % 2) * 4 + z, y * 2 + core, x // 2)


def along(axis, pos, place):
    x, y, z, core = place
    if axis == "x":
        x = pos
    elif axis == "y":
        y = pos
    else:
        z = pos
    return device(x, y, z, core)


def position(axis, place):
    return place["xyz".index(axis)]


def greet(devices):
    barrier = pltpu.get_barrier_semaphore()
    for dev in devices:
        pl.semaphore_signal(barrier, inc=1, device_id=dev, device_id_type=MESH)
    pl.semaphore_wait(barrier, len(devices))


def torus_peers(place):
    x, y, z, core = place
    peers = []
    for axis in "xyz":
        pos = position(axis, place)
        peers += [along(axis, (pos + d) % 4, place) for d in (1, 2, 3)]
    return peers + [device(x, y, z, 1 - core)]


class Wires:
    def __init__(self, send_sem, recv_sem):
        self.send_sem, self.recv_sem, self.used = send_sem, recv_sem, 0

    def take(self, count=1):
        self.used += count
        return self.used - count

    def copy(self, number, src, dst, dev):
        return pltpu.make_async_remote_copy(
            src_ref=src,
            dst_ref=dst,
            send_sem=self.send_sem.at[number],
            recv_sem=self.recv_sem.at[number],
            device_id=dev,
            device_id_type=MESH,
        )

    def send(self, number, src, dst, dev):
        copy = self.copy(number, src, dst, dev)
        copy.start()
        return copy


def each(dims, body, loop):
    if not loop or len(dims) < 2:
        body((EVERY,) * len(dims))
        return

    def step(i, _):
        body((i,) + (EVERY,) * (len(dims) - 1))
        return 0

    lax.fori_loop(0, 4, step, 0)


def put(index, dims, axis, pos):
    index = list(index)
    index.insert(dims.index(axis), pos)
    return tuple(index)


class Reduce:
    def __init__(
        self, place, wires, axis, dims, home, out, rows, lane, got, loop=False, direct=False
    ):
        self.axis, self.dims, self.home, self.out, self.rows, self.got = axis, dims, home, out, rows, got
        self.loop, self.direct = loop, direct
        self.across = along(axis, (position(axis, place) + 2) % 4, place)
        self.first, self.second = pl.ds(lane, 128), pl.ds(lane + 128, 128)
        self.rest = tuple(d for d in dims if d != axis)
        self.wires, self.base = wires, wires.take(6)
        me = position(axis, place)
        self.me, self.plus, self.minus, self.opposite = me, (me + 1) % 4, (me + 3) % 4, (me + 2) % 4
        self.up, self.down = along(axis, self.plus, place), along(axis, self.minus, place)
        self.copies = {}

    def go(self, slot, pos, lanes, dev):
        index = put([pl.ds(0, 4)] * len(self.rest), self.dims, self.axis, pos)
        src = self.out.at[index + (self.rows, lanes)]
        self.copies[slot] = self.wires.send(self.base + slot, src, self.got.at[slot], dev)

    def begin(self):
        self.go(0, self.opposite, self.first, self.across if self.direct else self.up)
        self.go(3, self.opposite, self.second, self.across if self.direct else self.down)

    def follow(self):
        self.go(1, self.plus, self.second, self.up)
        self.go(4, self.minus, self.first, self.down)
        if self.direct:
            self.go(2, self.plus, self.first, self.up)
            self.go(5, self.minus, self.second, self.down)

    def relay(self):
        if self.direct:
            return
        for slot, pos, lanes, dev in (
            (0, self.plus, self.first, self.up),
            (3, self.minus, self.second, self.down),
        ):
            self.copies[slot].wait_recv()

            def body(index):
                at = put(index, self.dims, self.axis, pos) + (self.rows, lanes)
                total = self.home[at] + self.got[(slot,) + index].astype(F32)
                self.out[at] = total.astype(self.out.dtype)

            each(self.rest, body, self.loop)
            self.go(slot + 2, pos, lanes, dev)

    def finish(self, store):
        for slot in (1, 4, 2, 5) + ((0, 3) if self.direct else ()):
            self.copies[slot].wait_recv()

        def body(index):
            for half, lanes, one, two in ((0, self.first, 2, 4), (1, self.second, 1, 5)):
                at = put(index, self.dims, self.axis, self.me) + (self.rows, lanes)
                total = self.home[at] + self.got[(one,) + index].astype(F32)
                total = total + self.got[(two,) + index].astype(F32)
                if self.direct:
                    total = total + self.got[(3 * half,) + index].astype(F32)
                store(index, half, total)

        each(self.rest, body, self.loop)
        for copy in self.copies.values():
            copy.wait_send()


class Gather:
    def __init__(self, place, wires, axis, ref, base, size, lanes, halves, mate=None):
        self.ref, self.base, self.size, self.mate = ref, base, size, mate
        self.lanes, self.halves = lanes, halves
        self.wires, self.first = wires, wires.take(10)
        me = position(axis, place)
        self.me, self.plus, self.minus, self.opposite = me, (me + 1) % 4, (me + 3) % 4, (me + 2) % 4
        self.up, self.down = along(axis, self.plus, place), along(axis, self.minus, place)
        self.across = along(axis, self.opposite, place)
        self.copies = []
        self.passed = []

    def go(self, slot, pos, lanes, dev):
        rows = pl.ds(pl.multiple_of(self.base + pos * self.size, self.size), self.size)
        part = self.ref.at[rows, lanes]
        return self.wires.send(self.first + slot, part, part, dev)

    def share(self, slot, pos):
        if self.mate is not None:
            self.passed.append(self.go(slot, pos, self.lanes, self.mate))

    def begin(self):
        if self.mate is None:
            for slot, dev in enumerate((self.across, self.up, self.down)):
                self.copies += [self.go(slot, self.me, self.lanes, dev)]
            return
        low, high = self.halves
        self.copies += [self.go(0, self.me, low, self.up), self.go(1, self.me, high, self.down)]
        self.copies += [self.go(8, self.me, high, self.up), self.go(9, self.me, low, self.down)]
        self.share(4, self.me)

    def relay(self):
        if self.mate is None:
            return
        low, high = self.halves
        self.copies[0].wait_recv()
        self.copies += [self.go(2, self.minus, low, self.up)]
        self.copies[1].wait_recv()
        self.copies += [self.go(3, self.plus, high, self.down)]

    def pass_on(self):
        if self.mate is None:
            return
        self.copies[2].wait_recv()
        self.copies[3].wait_recv()
        self.share(5, self.minus)
        self.share(6, self.plus)

    def arrive(self):
        if self.mate is None:
            for copy in self.copies:
                copy.wait_recv()
            return
        self.copies[4].wait_recv()
        self.copies[5].wait_recv()
        self.share(7, self.opposite)

    def finish(self):
        for copy in self.passed:
            copy.wait_recv()
        for copy in self.copies + self.passed:
            copy.wait_send()


def row_of(block, k):
    return jnp.broadcast_to(block[k : k + 1, :], block.shape)


def pieces(value, count):
    terms = []
    for _ in range(count):
        term = value.astype(BF16).astype(F32)
        terms.append(term)
        value = value - term
    return terms


def eliminate(rows, right, cols, sub):
    scale = jnp.zeros((8, 128), F32)
    for k in range(8):
        inv = 1.0 / row_of(cols[0][k], k)
        scale = jnp.where(sub == k, inv, scale)
        pivot_row = row_of(rows[0], k)
        pivot_right = row_of(right[0], k)
        heads = [row_of(cols[0][m], k) for m in range(k + 1, 8)]
        for t in range(len(rows)):
            mult = cols[t][k] * inv
            if t == 0:
                mult = jnp.where(sub > k, mult, 0.0)
            for i, m in enumerate(range(k + 1, 8)):
                cols[t][m] = cols[t][m] - mult * heads[i]
            rows[t] = rows[t] - mult * pivot_row
            right[t] = right[t] - mult * pivot_right
    return rows, right, scale


def stack_dot(left, right):
    a1, a2, a3 = pieces(left, 3)
    b1, b2, b3 = pieces(right, 3)
    a = jnp.concatenate([a1, a1, a2, a2, a1, a3], axis=0).astype(BF16)
    b = jnp.concatenate([b1, b2, b1, b2, b3, b1], axis=0).astype(BF16)
    return lax.dot_general(a, b, (((0,), (0,)), ((), ())), preferred_element_type=F32)


def factor_block(a_ref, x_ref, middle):
    sub = lax.broadcasted_iota(jnp.int32, (8, 128), 0)
    row = lax.broadcasted_iota(jnp.int32, (128, 128), 0)
    lane = lax.broadcasted_iota(jnp.int32, (128, 128), 1)
    x_ref[...] = jnp.where(row == lane, 1.0, 0.0).astype(F32)
    for g in range(16):
        b = g * 8
        n = 2 if g < 15 else 1
        rows = [a_ref[b + 8 * t : b + 8 * t + 8, :] for t in range(n)]
        right = [x_ref[b + 8 * t : b + 8 * t + 8, :] for t in range(n)]
        cols = [
            [jnp.broadcast_to(rows[t][:, b + m : b + m + 1], (8, 128)) for m in range(8)]
            for t in range(n)
        ]
        rows, right, scale = eliminate(rows, right, cols, sub)
        if n == 2:
            a_ref[b + 8 : b + 16, :] = rows[1]
            x_ref[b + 8 : b + 16, :] = right[1]
        if g < 14:
            low = b + 16
            both = jnp.concatenate([rows[0], right[0]], axis=1)
            change = stack_dot(rows[0] * scale, both)
            a_ref[low:, :] = a_ref[low:, :] - change[low:, :128]
            x_ref[low:, :] = x_ref[low:, :] - change[low:, 128:]
        x_ref[b : b + 8, :] = right[0] * jnp.sqrt(scale)
        middle(g)


def two(value):
    high = value.astype(BF16)
    return high, (value - high.astype(F32)).astype(BF16)


def dot_two(left, right):
    lh, ll = two(left)
    rh, rl = two(right)
    return jnp.dot(
        jnp.concatenate([lh, ll, lh], axis=1),
        jnp.concatenate([rh, rh, rl], axis=0),
        preferred_element_type=F32,
    )


def invert_factor(work, a_ref, x_ref, between):
    n = work.shape[0]
    for k in range(n // 128):
        b, e = k * 128, k * 128 + 128
        a_ref[...] = work[b:e, b:e]
        factor_block(a_ref, x_ref, between)
        inverse = x_ref[...]
        for low, high in ((0, b), (e, n)):
            if low < high:
                work[b:e, low:high] = dot_two(inverse, work[b:e, low:high])
        work[b:e, b:e] = inverse
        if e < n:
            high, low = two(work[b:e, :])
            left = jnp.concatenate([high[:, e:], low[:, e:], high[:, e:]], axis=0)
            both = jnp.concatenate([high, high, low], axis=0)
            change = lax.dot_general(
                left, both, (((0,), (0,)), ((), ())), preferred_element_type=F32
            )
            if b:
                work[e:, :b] = work[e:, :b] - change[:, :b]
            work[e:, b:e] = -change[:, b:e]
            work[e:, e:] = work[e:, e:] - change[:, e:]
        between(16)


DIMS = "xzy"
ORDERS = ("xyz", "yzx", "zxy")
LEAD_ORDERS = ("xyz", "yzx")
PARTS = ((0, 96), (96, 80), (176, 80))
CHUNKS = COLS // 128


def kernel(
    basis, classes, cond_table, ground_table, port_cells, port_load, tile, factor, other,
    cond, ground, panel, scaled, faces, halos, hz, image, image_t,
    lead_window, lead_home, lead_out, window, home, out, work, a_ref, x_ref, total, rows_t,
    *rest,
):
    lead_gots, lead_sums, gots, sums = rest[:6], rest[6:10], rest[10:19], rest[19:25]
    load_sem, send_sem, recv_sem = rest[25:]
    wires = Wires(send_sem, recv_sem)
    gx, gy, gz = lax.axis_index("gx"), lax.axis_index("gy"), lax.axis_index("gz")
    place = here()
    x, y, z, core = place
    mate = device(x, y, z, 1 - core)
    beside = [
        ((gx + 7) % 8, gy, gz),
        ((gx + 1) % 8, gy, gz),
        (gx, (gy + 7) % 8, gz),
        (gx, (gy + 1) % 8, gz),
        (gx, gy, 1 - gz),
    ]
    load = pltpu.make_async_copy(basis.at[:, pl.ds(0, COLS)], panel, load_sem.at[0])
    load.start()
    own_lead = []
    for rb in range(2):
        begin = pl.multiple_of(rb * 512 + core * 256, 256)
        own_lead.append(
            pltpu.make_async_copy(
                basis.at[:, pl.ds(begin, 256)],
                lead_window.at[pl.ds(0, 512), pl.ds(rb * 256, 256)],
                load_sem.at[1 + rb],
            )
        )
        own_lead[rb].start()
    greet(beside + torus_peers(place))

    swap_base = wires.take(16)

    def swap(rb, dst):
        begin = pl.multiple_of(rb * 512 + (1 - core) * 256, 256)
        return wires.copy(swap_base + rb, basis.at[:, pl.ds(begin, 256)], dst, mate)

    def far(rb):
        return other.at[:, pl.ds(pl.multiple_of(rb * 256, 256), 256)]

    lead_swaps = [
        swap(rb, lead_window.at[pl.ds(512, 512), pl.ds(rb * 256, 256)]) for rb in range(2)
    ]
    for copy in lead_swaps:
        copy.start()

    def look_up(i, _):
        kinds = classes[i]
        lane = lax.broadcasted_iota(jnp.int32, (8, 8), 1)
        diagonal = lane == lax.broadcasted_iota(jnp.int32, (8, 8), 0)
        for table, out_ref in ((cond_table, cond), (ground_table, ground)):
            values = jnp.zeros((8, 8), F32)
            for kind in range(16):
                values = jnp.where(kinds == kind, table[kind], values)
            columns = []
            for j in range(8):
                line = jnp.broadcast_to(values[j : j + 1, :], (8, 8))
                line = jnp.sum(jnp.where(diagonal, line, 0.0), axis=1, keepdims=True)
                columns.append(jnp.broadcast_to(line, (8, 128)))
            rows = pl.ds(pl.multiple_of(i * 64, 64), 64)
            out_ref[rows, :] = jnp.concatenate(columns, axis=0)
        return 0

    lax.fori_loop(0, 8, look_up, 0)
    load.wait()

    def scale(c, _):
        lanes = pl.ds(pl.multiple_of(c * 128, 128), 128)
        inner = lax.broadcasted_iota(jnp.int32, (8, 128), 0)
        y_low, y_high, z_face = [], [], []
        for i in range(8):
            rows = pl.ds(i * 64, 64)
            value = (cond[rows, :] * panel[rows, lanes].astype(F32)).astype(BF16)
            scaled[rows, lanes] = value
            if i == 0:
                faces[0, :, lanes] = value
            if i == 7:
                faces[1, :, lanes] = value
            value = value.astype(F32)
            y_low.append(value[:8])
            y_high.append(value[56:])
            face = jnp.zeros((8, 128), F32)
            for j in range(8):
                cell = value[j * 8 : j * 8 + 8]
                low = jnp.broadcast_to(cell[0:1, :], (8, 128))
                high = jnp.broadcast_to(cell[7:8, :], (8, 128))
                face = jnp.where(inner == j, jnp.where(gz == 1, low, high), face)
            z_face.append(face)
        for f, face in ((2, y_low), (3, y_high), (4, z_face)):
            faces[f, :, lanes] = jnp.concatenate(face, axis=0).astype(BF16)
        return 0

    lax.fori_loop(0, CHUNKS, scale, 0)
    lands = [1, 0, 3, 2, 4]
    face_base = wires.take(5)
    face_copies = [
        wires.send(face_base + f, faces.at[f], halos.at[lands[f]], beside[f]) for f in range(5)
    ]

    def start_swap(rb, _):
        swap(rb, far(rb)).start()
        return 0

    lax.fori_loop(2, 16, start_swap, 0)
    def add_ports(i, _):
        row = lax.broadcasted_iota(jnp.int32, (64, 128), 0)
        flat = ((gx * 8 + i) * 64 + gy * 8 + row // 8) * 16 + gz * 8 + row % 8
        found = jnp.zeros((64, 128), F32)
        for j in range(16):
            match = flat == jnp.broadcast_to(port_cells[j : j + 1, :], (64, 128))
            found = found + jnp.where(match, jnp.broadcast_to(port_load[j : j + 1, :], (64, 128)), 0.0)
        rows = pl.ds(pl.multiple_of(i * 64, 64), 64)
        ground[rows, :] = ground[rows, :] + jnp.sum(found, axis=1, keepdims=True)
        return 0

    lax.fori_loop(0, 8, add_ports, 0)
    for copy in face_copies:
        copy.wait()

    keep = [gx > 0, gx < 7, gy > 0, gy < 7]
    image_base = wires.take(CHUNKS)

    def image_copy(c):
        lanes = pl.ds(pl.multiple_of(c * 128, 128), 128)
        return wires.copy(
            image_base + c, image.at[pl.ds(0, 512), lanes], image.at[pl.ds(512, 512), lanes], mate
        )

    def stencil(c, _):
        lanes = pl.ds(pl.multiple_of(c * 128, 128), 128)
        inner = lax.broadcasted_iota(jnp.int32, (64, 128), 0) % 8

        def halo(f):
            return jnp.where(keep[f], halos[f, :, lanes].astype(F32), 0.0)

        hz[...] = halos[4, :, lanes].astype(F32)
        x_low, x_high, y_low, y_high = halo(0), halo(1), halo(2), halo(3)
        for i in range(8):
            rows = pl.ds(i * 64, 64)
            me = scaled[rows, lanes].astype(F32)
            down = scaled[pl.ds((i - 1) * 64, 64), lanes].astype(F32) if i > 0 else x_low
            up = scaled[pl.ds((i + 1) * 64, 64), lanes].astype(F32) if i < 7 else x_high
            around = up + down
            around = around + jnp.concatenate([me[8:], y_high[i * 8 : i * 8 + 8]], axis=0)
            around = around + jnp.concatenate([y_low[i * 8 : i * 8 + 8], me[:56]], axis=0)
            ends = jnp.concatenate(
                [jnp.broadcast_to(hz[i * 8 + j : i * 8 + j + 1, :], (8, 128)) for j in range(8)],
                axis=0,
            )
            high = pltpu.roll(me, 63, 0)
            low = pltpu.roll(me, 1, 0)
            high = jnp.where(inner == 7, jnp.where(gz == 0, ends, 0.0), high)
            low = jnp.where(inner == 0, jnp.where(gz == 1, ends, 0.0), low)
            around = around + high + low
            value = cond[rows, :] * (6.0 * me - around)
            value = value + ground[rows, :] * panel[rows, lanes].astype(F32)
            image[rows, lanes] = value.astype(BF16)
        image_copy(c).start()
        return 0

    lax.fori_loop(0, CHUNKS, stencil, 0)

    def turn(c, _):
        image_copy(c).wait()
        rows = pl.ds(pl.multiple_of(c * 128, 128), 128)
        image_t[rows, :] = image[:, rows].T
        return 0

    lax.fori_loop(0, CHUNKS, turn, 0)

    for copy in own_lead + lead_swaps:
        copy.wait()

    def lead_terms(c, _):
        rows = pl.ds(pl.multiple_of(c * 256, 256), 256)
        product = jnp.dot(image_t[rows, :], lead_window[...], preferred_element_type=F32)
        for i in range(16):
            value = product[i * 16 : i * 16 + 16, :]
            lead_home[c, i // 4, i % 4] = value
            lead_out[c, i // 4, i % 4] = value.astype(BF16)
        return 0

    lax.fori_loop(0, 4, lead_terms, 0)

    def fetch(rb):
        slot = rb % 2
        begin = pl.multiple_of(rb * 512 + core * 256, 256)
        return (
            pltpu.make_async_copy(
                basis.at[:, pl.ds(begin, 256)],
                window.at[slot, pl.ds(0, 512), :],
                load_sem.at[3 + slot],
            ),
            pltpu.make_async_copy(
                far(rb), window.at[slot, pl.ds(512, 512), :], load_sem.at[5 + slot]
            ),
        )

    def start_fetch(rb):
        swap(rb, far(rb)).wait()
        for copy in fetch(rb):
            copy.start()

    def multiply(rb, read):
        to_x, to_z = (rb % 2) * 2 + rb // 8, (rb // 2) % 4

        def one(c, _):
            rows = pl.ds(pl.multiple_of(c * 256, 256), 256)
            product = jnp.dot(image_t[rows, :], read(), preferred_element_type=F32)
            home[to_x, to_z, c] = product
            out[to_x, to_z, c] = product.astype(BF16)
            return 0

        lax.fori_loop(0, 4, one, 0)

    def terms(low, high):
        def one(rb, _):
            for copy in fetch(rb):
                copy.wait()

            @pl.when(rb < 15)
            def _():
                start_fetch(rb + 1)

            multiply(rb, lambda: window[rb % 2])
            return 0

        lax.fori_loop(low, high, one, 0)

    def lead_block(rb):
        multiply(rb, lambda: lead_window[:, rb * 256 : rb * 256 + 256])

    dims = [LEAD_ORDERS[p] for p in range(2)]
    homes, outs, lane = [lead_home] * 2, [lead_out] * 2, [0, 256]
    for stage in range(3):
        steps = [
            Reduce(
                place, wires, LEAD_ORDERS[p][stage], dims[p], homes[p], outs[p], EVERY, lane[p],
                lead_gots[p * 3 + stage], direct=stage > 0,
            )
            for p in range(2)
        ]
        for step in steps:
            step.begin()
        for step in steps:
            step.follow()
        if stage == 0:
            start_fetch(2)
            lead_block(0)
            lead_block(1)
        else:
            terms(5 * stage, 5 * stage + 2)
        for step in steps:
            step.relay()
        if stage == 0:
            terms(2, 5)
        else:
            terms(5 * stage + 2, 5 * stage + 5)
        for p, step in enumerate(steps):
            if stage < 2:
                acc = lead_sums[p * 2 + stage]

                def store(index, half, value, acc=acc):
                    acc[index + (EVERY, pl.ds(half * 128, 128))] = value

                homes[p] = outs[p] = acc
                lane[p] = 0
            else:
                at = [position(axis, place) for axis in LEAD_ORDERS[p]]
                rows = pl.ds(pl.multiple_of((at[0] * 16 + at[1] * 4 + at[2]) * 16, 16), 16)

                def store(index, half, value, p=p, rows=rows):
                    begin = pl.multiple_of(p * 512 + core * 256 + half * 128, 128)
                    work[rows, pl.ds(begin, 128)] = value

            step.finish(store)
            dims[p] = step.rest
    def gather_rows():
        slots = [2 * ((y + d) % 4) + core for d in range(4)]
        up, down = along("y", (y + 1) % 4, place), along("y", (y + 3) % 4, place)
        base = wires.take(10)

        def go(number, slot, lanes, dev):
            block = rows_t.at[pl.ds(pl.multiple_of(slot * 128, 128), 128), lanes]
            return wires.send(base + number, block, block, dev)

        whole, low, high = pl.ds(0, 512), pl.ds(0, 256), pl.ds(256, 256)
        one, two = go(0, slots[0], low, up), go(1, slots[0], high, down)
        three, four = go(8, slots[0], high, up), go(9, slots[0], low, down)
        passed = [go(4, slots[0], whole, mate)]
        yield
        one.wait_recv()
        five = go(2, slots[3], low, up)
        two.wait_recv()
        six = go(3, slots[1], high, down)
        yield
        three.wait_recv()
        passed += [go(5, slots[3], whole, mate)]
        four.wait_recv()
        passed += [go(6, slots[1], whole, mate)]
        five.wait_recv()
        six.wait_recv()
        passed += [go(7, slots[2], whole, mate)]
        for copy in passed:
            copy.wait_recv()
        for copy in passed + [one, two, three, four, five, six]:
            copy.wait_send()

    def all_rows():
        dims, rows = [DIMS] * 3, [pl.ds(begin, size) for begin, size in PARTS]
        homes, outs = [home] * 3, [out] * 3
        for stage in range(3):
            steps = [
                Reduce(
                    place, wires, ORDERS[p][stage], dims[p], homes[p], outs[p], rows[p], 0,
                    gots[p * 3 + stage], loop=True, direct=stage == 2,
                )
                for p in range(3)
            ]
            for step in steps:
                step.begin()
            if stage == 0:
                yield
            for step in steps:
                step.follow()
            yield
            if stage < 2:
                for step in steps:
                    step.relay()
                yield
            for p, step in enumerate(steps):
                if stage < 2:
                    acc = sums[p * 2 + stage]

                    def store(index, half, value, acc=acc):
                        acc[index + (EVERY, pl.ds(half * 128, 128))] = value

                    homes[p] = outs[p] = acc
                    rows[p] = EVERY
                else:

                    def store(index, half, value, p=p):
                        total[pl.ds(*PARTS[p]), pl.ds(half * 128, 128)] = value

                step.finish(store)
                dims[p] = step.rest
        mine = pl.ds(pl.multiple_of(core * 128, 128), 128)
        theirs = pl.ds(pl.multiple_of((1 - core) * 128, 128), 128)
        lanes = pl.ds(pl.multiple_of(core * 256, 256), 256)
        swapped = wires.send(wires.take(), total.at[theirs, :], tile.at[:, lanes], mate)
        tile[:, lanes] = total[mine, :]
        yield
        swapped.wait()
        rows_t[pl.ds(pl.multiple_of(gy * 128, 128), 128), :] = tile[...]
        yield from gather_rows()

    events = all_rows()

    for stage in range(3):
        steps = []
        for p in range(2):
            at = [position(axis, place) for axis in LEAD_ORDERS[p]]
            base = (at[0] * 256 + at[1] * 64, at[0] * 256, 0)[stage]
            begin = pl.multiple_of(p * 512 + core * 256, 256)
            halves = [pl.ds(begin, 128), pl.ds(pl.multiple_of(begin + 128, 128), 128)]
            steps.append(
                Gather(
                    place, wires, LEAD_ORDERS[p][2 - stage], work, base, (16, 64, 256)[stage],
                    pl.ds(begin, 256), halves, mate if stage == 2 else None,
                )
            )
        for step in steps:
            step.begin()
        if stage == 0:
            terms(15, 16)
        for _ in range(AHEAD[2 * stage]):
            next(events)
        for step in steps:
            step.relay()
        for step in steps:
            step.pass_on()
        for _ in range(AHEAD[2 * stage + 1]):
            next(events)
        if stage < 2:
            for step in steps:
                step.arrive()
                step.finish()

    for step in steps:
        step.arrive()
    for step in steps:
        step.finish()
    for b in range(0, COLS, NB):
        block = work[b : b + NB, b : b + NB]
        work[b : b + NB, b : b + NB] = 0.5 * (block + block.T)
    count = [0]

    def between(_):
        if count[0] in WHEN:
            next(events)
        count[0] += 1

    invert_factor(work, a_ref, x_ref, between)
    for _ in events:
        pass
    block = work[pl.ds(pl.multiple_of(gy * 128, 128), 128), :]
    lane = lax.broadcasted_iota(jnp.int32, block.shape, 1)
    block = jnp.where(lane < (gy + 1) * 128, block, 0.0)
    mine = dot_two(block, rows_t[...])
    column = gy * 128 + lax.broadcasted_iota(jnp.int32, mine.shape, 0)
    row = (gx * 2 + gz) * 512 + lax.broadcasted_iota(jnp.int32, mine.shape, 1)
    factor[...] = jnp.where(column <= row, mine, 0.0)


AHEAD = (1, 0, 1, 0, 0, 1)
WHEN = (34, 55, 80, 98, 105, 122)
WIRES = 200


def project(basis, classes, cond_table, ground_table, port_cells, port_load):
    any_spec = pl.BlockSpec(memory_space=pltpu.HBM)
    vmem = pl.BlockSpec(memory_space=pltpu.VMEM)
    smem = pl.BlockSpec(memory_space=pltpu.SMEM)
    lead_gots, lead_sums, gots, sums = [], [], [], []
    for _ in range(2):
        lead_gots += [
            pltpu.VMEM((6, 4, 4, 16, 128), BF16),
            pltpu.VMEM((6, 4, 16, 128), F32),
            pltpu.VMEM((6, 16, 128), F32),
        ]
        lead_sums += [pltpu.VMEM((4, 4, 16, 256), F32), pltpu.VMEM((4, 16, 256), F32)]
    for _, size in PARTS:
        gots += [
            pltpu.VMEM((6, 4, 4, size, 128), BF16),
            pltpu.VMEM((6, 4, size, 128), F32),
            pltpu.VMEM((6, size, 128), F32),
        ]
        sums += [pltpu.VMEM((4, 4, size, 256), F32), pltpu.VMEM((4, size, 256), F32)]
    return pl.pallas_call(
        kernel,
        out_shape=(
            jax.ShapeDtypeStruct((128, 512), F32),
            jax.ShapeDtypeStruct((128, 512), F32),
            jax.ShapeDtypeStruct((512, 4096), BF16),
        ),
        in_specs=[any_spec, vmem, smem, smem, vmem, vmem],
        out_specs=(vmem, vmem, any_spec),
        scratch_shapes=[
            pltpu.VMEM((512, 128), F32),
            pltpu.VMEM((512, 128), F32),
            pltpu.VMEM((512, COLS), BF16),
            pltpu.VMEM((512, COLS), BF16),
            pltpu.VMEM((5, 64, COLS), BF16),
            pltpu.VMEM((5, 64, COLS), BF16),
            pltpu.VMEM((64, 128), F32),
            pltpu.VMEM((1024, COLS), BF16),
            pltpu.VMEM((COLS, 1024), BF16),
            pltpu.VMEM((1024, 512), BF16),
            pltpu.VMEM((4, 4, 4, 16, 512), F32),
            pltpu.VMEM((4, 4, 4, 16, 512), BF16),
            pltpu.VMEM((2, 1024, 256), BF16),
            pltpu.VMEM((4, 4, 4, 256, 256), F32),
            pltpu.VMEM((4, 4, 4, 256, 256), BF16),
            pltpu.VMEM((COLS, COLS), F32),
            pltpu.VMEM((128, 128), F32),
            pltpu.VMEM((128, 128), F32),
            pltpu.VMEM((256, 256), F32),
            pltpu.VMEM((COLS, 512), F32),
            *lead_gots,
            *lead_sums,
            *gots,
            *sums,
            pltpu.SemaphoreType.DMA((7,)),
            pltpu.SemaphoreType.DMA((WIRES,)),
            pltpu.SemaphoreType.DMA((WIRES,)),
        ],
        compiler_params=pltpu.CompilerParams(
            collective_id=0, has_side_effects=True, vmem_limit_bytes=67043328
        ),
        name="project",
    )(basis, classes, cond_table, ground_table, port_cells, port_load)


def turn_kernel(tile, factor, tile_out, factor_out):
    tile_out[...] = tile[...].T
    factor_out[...] = factor[...].T


def local(basis, classes, cond_table, ground_table, port_cells, port_load):
    flat = basis.reshape(512, basis.shape[3])
    tile, factor, _ = project(
        flat, classes, cond_table, ground_table, port_cells.reshape(16, 128), port_load.reshape(16, 128)
    )
    shape = jax.ShapeDtypeStruct((512, 128), F32)
    return pl.pallas_call(turn_kernel, out_shape=(shape, shape), name="turn")(tile, factor)


def solution(mesh):
    placed = (P("gx", "gy", "gz", None), P("gx", "gy", "gz"), P(), P(), P(), P())
    return jax.shard_map(
        local,
        mesh=mesh,
        in_specs=placed,
        out_specs=(P(("gx", "gz"), "gy"), P(("gx", "gz"), "gy")),
        check_vma=False,
    )
```

```python
import jax
import jax.numpy as jnp
from jax import lax
from jax.experimental import pallas as pl
from jax.experimental.pallas import tpu as pltpu
from jax.sharding import PartitionSpec as P

NB = 512
PANELS = 2
COLS = NB * PANELS
F32 = jnp.float32
BF16 = jnp.bfloat16
MESH = pl.DeviceIdType.MESH
EVERY = slice(None)


def here():
    gx, gy, gz = lax.axis_index("gx"), lax.axis_index("gy"), lax.axis_index("gz")
    return gz * 2 + gx // 4, gy // 2, gx % 4, gy % 2


def device(x, y, z, core):
    return ((x % 2) * 4 + z, y * 2 + core, x // 2)


def along(axis, pos, place):
    x, y, z, core = place
    if axis == "x":
        x = pos
    elif axis == "y":
        y = pos
    else:
        z = pos
    return device(x, y, z, core)


def position(axis, place):
    return place["xyz".index(axis)]


def greet(devices):
    barrier = pltpu.get_barrier_semaphore()
    for dev in devices:
        pl.semaphore_signal(barrier, inc=1, device_id=dev, device_id_type=MESH)
    pl.semaphore_wait(barrier, len(devices))


def torus_peers(place):
    x, y, z, core = place
    peers = []
    for axis in "xyz":
        pos = position(axis, place)
        peers += [along(axis, (pos + d) % 4, place) for d in (1, 2, 3)]
    return peers + [device(x, y, z, 1 - core)]


class Wires:
    def __init__(self, send_sem, recv_sem):
        self.send_sem, self.recv_sem, self.used = send_sem, recv_sem, 0

    def take(self, count=1):
        self.used += count
        return self.used - count

    def copy(self, number, src, dst, dev):
        return pltpu.make_async_remote_copy(
            src_ref=src,
            dst_ref=dst,
            send_sem=self.send_sem.at[number],
            recv_sem=self.recv_sem.at[number],
            device_id=dev,
            device_id_type=MESH,
        )

    def send(self, number, src, dst, dev):
        copy = self.copy(number, src, dst, dev)
        copy.start()
        return copy


def each(dims, body, loop):
    if not loop or len(dims) < 2:
        body((EVERY,) * len(dims))
        return

    def step(i, _):
        body((i,) + (EVERY,) * (len(dims) - 1))
        return 0

    lax.fori_loop(0, 4, step, 0)


def put(index, dims, axis, pos):
    index = list(index)
    index.insert(dims.index(axis), pos)
    return tuple(index)


class Reduce:
    def __init__(
        self, place, wires, axis, dims, home, out, rows, lane, got, loop=False, direct=False
    ):
        self.axis, self.dims, self.home, self.out, self.rows, self.got = axis, dims, home, out, rows, got
        self.loop, self.direct = loop, direct
        self.across = along(axis, (position(axis, place) + 2) % 4, place)
        self.first, self.second = pl.ds(lane, 128), pl.ds(lane + 128, 128)
        self.rest = tuple(d for d in dims if d != axis)
        self.wires, self.base = wires, wires.take(6)
        me = position(axis, place)
        self.me, self.plus, self.minus, self.opposite = me, (me + 1) % 4, (me + 3) % 4, (me + 2) % 4
        self.up, self.down = along(axis, self.plus, place), along(axis, self.minus, place)
        self.copies = {}

    def go(self, slot, pos, lanes, dev):
        index = put([pl.ds(0, 4)] * len(self.rest), self.dims, self.axis, pos)
        src = self.out.at[index + (self.rows, lanes)]
        self.copies[slot] = self.wires.send(self.base + slot, src, self.got.at[slot], dev)

    def begin(self):
        self.go(0, self.opposite, self.first, self.across if self.direct else self.up)
        self.go(3, self.opposite, self.second, self.across if self.direct else self.down)

    def follow(self):
        self.go(1, self.plus, self.second, self.up)
        self.go(4, self.minus, self.first, self.down)
        if self.direct:
            self.go(2, self.plus, self.first, self.up)
            self.go(5, self.minus, self.second, self.down)

    def relay(self):
        if self.direct:
            return
        for slot, pos, lanes, dev in (
            (0, self.plus, self.first, self.up),
            (3, self.minus, self.second, self.down),
        ):
            self.copies[slot].wait_recv()

            def body(index):
                at = put(index, self.dims, self.axis, pos) + (self.rows, lanes)
                total = self.home[at] + self.got[(slot,) + index].astype(F32)
                self.out[at] = total.astype(self.out.dtype)

            each(self.rest, body, self.loop)
            self.go(slot + 2, pos, lanes, dev)

    def finish(self, store):
        for slot in (1, 4, 2, 5) + ((0, 3) if self.direct else ()):
            self.copies[slot].wait_recv()

        def body(index):
            for half, lanes, one, two in ((0, self.first, 2, 4), (1, self.second, 1, 5)):
                at = put(index, self.dims, self.axis, self.me) + (self.rows, lanes)
                total = self.home[at] + self.got[(one,) + index].astype(F32)
                total = total + self.got[(two,) + index].astype(F32)
                if self.direct:
                    total = total + self.got[(3 * half,) + index].astype(F32)
                store(index, half, total)

        each(self.rest, body, self.loop)
        for copy in self.copies.values():
            copy.wait_send()


class Gather:
    def __init__(self, place, wires, axis, ref, base, size, lanes, halves, mate=None, relayed=False):
        self.ref, self.base, self.size, self.mate = ref, base, size, mate
        self.lanes, self.halves = lanes, halves
        self.wires, self.first = wires, wires.take(10)
        me = position(axis, place)
        self.me, self.plus, self.minus, self.opposite = me, (me + 1) % 4, (me + 3) % 4, (me + 2) % 4
        self.up, self.down = along(axis, self.plus, place), along(axis, self.minus, place)
        self.across = along(axis, self.opposite, place)
        self.direct = mate is None and not relayed
        self.copies = []
        self.passed = []

    def go(self, slot, pos, lanes, dev):
        rows = pl.ds(pl.multiple_of(self.base + pos * self.size, self.size), self.size)
        part = self.ref.at[rows, lanes]
        return self.wires.send(self.first + slot, part, part, dev)

    def share(self, slot, pos):
        if self.mate is not None:
            self.passed.append(self.go(slot, pos, self.lanes, self.mate))

    def begin(self):
        if self.direct:
            for slot, dev in enumerate((self.across, self.up, self.down)):
                self.copies += [self.go(slot, self.me, self.lanes, dev)]
            return
        low, high = self.halves
        self.copies += [self.go(0, self.me, low, self.up), self.go(1, self.me, high, self.down)]
        self.copies += [self.go(8, self.me, high, self.up), self.go(9, self.me, low, self.down)]
        self.share(4, self.me)

    def relay(self):
        if self.direct:
            return
        low, high = self.halves
        self.copies[0].wait_recv()
        self.copies += [self.go(2, self.minus, low, self.up)]
        self.copies[1].wait_recv()
        self.copies += [self.go(3, self.plus, high, self.down)]

    def pass_on(self):
        if self.direct:
            return
        self.copies[2].wait_recv()
        self.copies[3].wait_recv()
        self.share(5, self.minus)
        self.share(6, self.plus)

    def arrive(self):
        if self.direct:
            for copy in self.copies:
                copy.wait_recv()
            return
        self.copies[4].wait_recv()
        self.copies[5].wait_recv()
        self.share(7, self.opposite)

    def finish(self):
        for copy in self.passed:
            copy.wait_recv()
        for copy in self.copies + self.passed:
            copy.wait_send()


def row_of(block, k):
    return jnp.broadcast_to(block[k : k + 1, :], block.shape)


def pieces(value, count):
    terms = []
    for _ in range(count):
        term = value.astype(BF16).astype(F32)
        terms.append(term)
        value = value - term
    return terms


def eliminate(rows, right, cols, sub):
    scale = jnp.zeros((8, 128), F32)
    for k in range(8):
        inv = 1.0 / row_of(cols[0][k], k)
        scale = jnp.where(sub == k, inv, scale)
        pivot_row = row_of(rows[0], k)
        pivot_right = row_of(right[0], k)
        heads = [row_of(cols[0][m], k) for m in range(k + 1, 8)]
        for t in range(len(rows)):
            mult = cols[t][k] * inv
            if t == 0:
                mult = jnp.where(sub > k, mult, 0.0)
            for i, m in enumerate(range(k + 1, 8)):
                cols[t][m] = cols[t][m] - mult * heads[i]
            rows[t] = rows[t] - mult * pivot_row
            right[t] = right[t] - mult * pivot_right
    return rows, right, scale


def stack_dot(left, right):
    a1, a2, a3 = pieces(left, 3)
    b1, b2, b3 = pieces(right, 3)
    a = jnp.concatenate([a1, a1, a2, a2, a1, a3], axis=0).astype(BF16)
    b = jnp.concatenate([b1, b2, b1, b2, b3, b1], axis=0).astype(BF16)
    return lax.dot_general(a, b, (((0,), (0,)), ((), ())), preferred_element_type=F32)


def factor_block(a_ref, x_ref, middle):
    sub = lax.broadcasted_iota(jnp.int32, (8, 128), 0)
    row = lax.broadcasted_iota(jnp.int32, (128, 128), 0)
    lane = lax.broadcasted_iota(jnp.int32, (128, 128), 1)
    x_ref[...] = jnp.where(row == lane, 1.0, 0.0).astype(F32)
    for g in range(16):
        b = g * 8
        n = 2 if g < 15 else 1
        rows = [a_ref[b + 8 * t : b + 8 * t + 8, :] for t in range(n)]
        right = [x_ref[b + 8 * t : b + 8 * t + 8, :] for t in range(n)]
        cols = [
            [jnp.broadcast_to(rows[t][:, b + m : b + m + 1], (8, 128)) for m in range(8)]
            for t in range(n)
        ]
        rows, right, scale = eliminate(rows, right, cols, sub)
        if n == 2:
            a_ref[b + 8 : b + 16, :] = rows[1]
            x_ref[b + 8 : b + 16, :] = right[1]
        if g < 14:
            low = b + 16
            both = jnp.concatenate([rows[0], right[0]], axis=1)
            change = stack_dot(rows[0] * scale, both)
            a_ref[low:, :] = a_ref[low:, :] - change[low:, :128]
            x_ref[low:, :] = x_ref[low:, :] - change[low:, 128:]
        x_ref[b : b + 8, :] = right[0] * jnp.sqrt(scale)
        middle(g)


def two(value):
    high = value.astype(BF16)
    return high, (value - high.astype(F32)).astype(BF16)


def dot_two(left, right):
    lh, ll = two(left)
    rh, rl = two(right)
    return jnp.dot(
        jnp.concatenate([lh, ll, lh], axis=1),
        jnp.concatenate([rh, rh, rl], axis=0),
        preferred_element_type=F32,
    )


def invert_factor(work, a_ref, x_ref, between):
    n = work.shape[0]
    for k in range(n // 128):
        b, e = k * 128, k * 128 + 128
        a_ref[...] = work[b:e, b:e]
        factor_block(a_ref, x_ref, between)
        inverse = x_ref[...]
        for low, high in ((0, b), (e, n)):
            if low < high:
                work[b:e, low:high] = dot_two(inverse, work[b:e, low:high])
        work[b:e, b:e] = inverse
        if e < n:
            high, low = two(work[b:e, :])
            left = jnp.concatenate([high[:, e:], low[:, e:], high[:, e:]], axis=0)
            both = jnp.concatenate([high, high, low], axis=0)
            change = lax.dot_general(
                left, both, (((0,), (0,)), ((), ())), preferred_element_type=F32
            )
            if b:
                work[e:, :b] = work[e:, :b] - change[:, :b]
            work[e:, b:e] = -change[:, b:e]
            work[e:, e:] = work[e:, e:] - change[:, e:]
        between(16)


DIMS = "xzy"
ORDERS = ("xyz", "yzx", "zxy")
LEAD_ORDERS = ("xyz", "yzx")
PARTS = ((0, 96), (96, 80), (176, 80))
CHUNKS = COLS // 128


def kernel(
    basis, classes, cond_table, ground_table, port_cells, port_load, tile, factor, other,
    cond, ground, panel, scaled, faces, halos, hz, image, image_t,
    lead_window, lead_home, lead_out, window, home, out, work, a_ref, x_ref, total, rows_t,
    *rest,
):
    lead_gots, lead_sums, gots, sums = rest[:6], rest[6:10], rest[10:19], rest[19:25]
    load_sem, send_sem, recv_sem = rest[25:]
    wires = Wires(send_sem, recv_sem)
    gx, gy, gz = lax.axis_index("gx"), lax.axis_index("gy"), lax.axis_index("gz")
    place = here()
    x, y, z, core = place
    mate = device(x, y, z, 1 - core)
    beside = [
        ((gx + 7) % 8, gy, gz),
        ((gx + 1) % 8, gy, gz),
        (gx, (gy + 7) % 8, gz),
        (gx, (gy + 1) % 8, gz),
        (gx, gy, 1 - gz),
    ]
    load = pltpu.make_async_copy(basis.at[:, pl.ds(0, COLS)], panel, load_sem.at[0])
    load.start()
    own_lead = []
    for rb in range(2):
        begin = pl.multiple_of(rb * 512 + core * 256, 256)
        own_lead.append(
            pltpu.make_async_copy(
                basis.at[:, pl.ds(begin, 256)],
                lead_window.at[pl.ds(0, 512), pl.ds(rb * 256, 256)],
                load_sem.at[1 + rb],
            )
        )
        own_lead[rb].start()
    greet(beside + torus_peers(place))

    swap_base = wires.take(16)

    def swap(rb, dst):
        begin = pl.multiple_of(rb * 512 + (1 - core) * 256, 256)
        return wires.copy(swap_base + rb, basis.at[:, pl.ds(begin, 256)], dst, mate)

    def far(rb):
        return other.at[:, pl.ds(pl.multiple_of(rb * 256, 256), 256)]

    lead_swaps = [
        swap(rb, lead_window.at[pl.ds(512, 512), pl.ds(rb * 256, 256)]) for rb in range(2)
    ]
    for copy in lead_swaps:
        copy.start()

    def look_up(i, _):
        kinds = classes[i]
        lane = lax.broadcasted_iota(jnp.int32, (8, 8), 1)
        diagonal = lane == lax.broadcasted_iota(jnp.int32, (8, 8), 0)
        for table, out_ref in ((cond_table, cond), (ground_table, ground)):
            values = jnp.zeros((8, 8), F32)
            for kind in range(16):
                values = jnp.where(kinds == kind, table[kind], values)
            columns = []
            for j in range(8):
                line = jnp.broadcast_to(values[j : j + 1, :], (8, 8))
                line = jnp.sum(jnp.where(diagonal, line, 0.0), axis=1, keepdims=True)
                columns.append(jnp.broadcast_to(line, (8, 128)))
            rows = pl.ds(pl.multiple_of(i * 64, 64), 64)
            out_ref[rows, :] = jnp.concatenate(columns, axis=0)
        return 0

    lax.fori_loop(0, 8, look_up, 0)
    load.wait()

    def scale(c, _):
        lanes = pl.ds(pl.multiple_of(c * 128, 128), 128)
        inner = lax.broadcasted_iota(jnp.int32, (8, 128), 0)
        y_low, y_high, z_face = [], [], []
        for i in range(8):
            rows = pl.ds(i * 64, 64)
            value = (cond[rows, :] * panel[rows, lanes].astype(F32)).astype(BF16)
            scaled[rows, lanes] = value
            if i == 0:
                faces[0, :, lanes] = value
            if i == 7:
                faces[1, :, lanes] = value
            value = value.astype(F32)
            y_low.append(value[:8])
            y_high.append(value[56:])
            face = jnp.zeros((8, 128), F32)
            for j in range(8):
                cell = value[j * 8 : j * 8 + 8]
                low = jnp.broadcast_to(cell[0:1, :], (8, 128))
                high = jnp.broadcast_to(cell[7:8, :], (8, 128))
                face = jnp.where(inner == j, jnp.where(gz == 1, low, high), face)
            z_face.append(face)
        for f, face in ((2, y_low), (3, y_high), (4, z_face)):
            faces[f, :, lanes] = jnp.concatenate(face, axis=0).astype(BF16)
        return 0

    lax.fori_loop(0, CHUNKS, scale, 0)
    lands = [1, 0, 3, 2, 4]
    face_base = wires.take(5)
    face_copies = [
        wires.send(face_base + f, faces.at[f], halos.at[lands[f]], beside[f]) for f in range(5)
    ]

    def start_swap(rb, _):
        swap(rb, far(rb)).start()
        return 0

    lax.fori_loop(2, 16, start_swap, 0)
    def add_ports(i, _):
        row = lax.broadcasted_iota(jnp.int32, (64, 128), 0)
        flat = ((gx * 8 + i) * 64 + gy * 8 + row // 8) * 16 + gz * 8 + row % 8
        found = jnp.zeros((64, 128), F32)
        for j in range(16):
            match = flat == jnp.broadcast_to(port_cells[j : j + 1, :], (64, 128))
            found = found + jnp.where(match, jnp.broadcast_to(port_load[j : j + 1, :], (64, 128)), 0.0)
        rows = pl.ds(pl.multiple_of(i * 64, 64), 64)
        ground[rows, :] = ground[rows, :] + jnp.sum(found, axis=1, keepdims=True)
        return 0

    lax.fori_loop(0, 8, add_ports, 0)
    for copy in face_copies:
        copy.wait()

    keep = [gx > 0, gx < 7, gy > 0, gy < 7]
    image_base = wires.take(CHUNKS)

    def image_copy(c):
        lanes = pl.ds(pl.multiple_of(c * 128, 128), 128)
        return wires.copy(
            image_base + c, image.at[pl.ds(0, 512), lanes], image.at[pl.ds(512, 512), lanes], mate
        )

    def stencil(c, _):
        lanes = pl.ds(pl.multiple_of(c * 128, 128), 128)
        inner = lax.broadcasted_iota(jnp.int32, (64, 128), 0) % 8

        def halo(f):
            return jnp.where(keep[f], halos[f, :, lanes].astype(F32), 0.0)

        hz[...] = halos[4, :, lanes].astype(F32)
        x_low, x_high, y_low, y_high = halo(0), halo(1), halo(2), halo(3)
        for i in range(8):
            rows = pl.ds(i * 64, 64)
            me = scaled[rows, lanes].astype(F32)
            down = scaled[pl.ds((i - 1) * 64, 64), lanes].astype(F32) if i > 0 else x_low
            up = scaled[pl.ds((i + 1) * 64, 64), lanes].astype(F32) if i < 7 else x_high
            around = up + down
            around = around + jnp.concatenate([me[8:], y_high[i * 8 : i * 8 + 8]], axis=0)
            around = around + jnp.concatenate([y_low[i * 8 : i * 8 + 8], me[:56]], axis=0)
            ends = jnp.concatenate(
                [jnp.broadcast_to(hz[i * 8 + j : i * 8 + j + 1, :], (8, 128)) for j in range(8)],
                axis=0,
            )
            high = pltpu.roll(me, 63, 0)
            low = pltpu.roll(me, 1, 0)
            high = jnp.where(inner == 7, jnp.where(gz == 0, ends, 0.0), high)
            low = jnp.where(inner == 0, jnp.where(gz == 1, ends, 0.0), low)
            around = around + high + low
            value = cond[rows, :] * (6.0 * me - around)
            value = value + ground[rows, :] * panel[rows, lanes].astype(F32)
            image[rows, lanes] = value.astype(BF16)
        image_copy(c).start()
        return 0

    lax.fori_loop(0, CHUNKS, stencil, 0)

    def turn(c, _):
        image_copy(c).wait()
        rows = pl.ds(pl.multiple_of(c * 128, 128), 128)
        image_t[rows, :] = image[:, rows].T
        return 0

    lax.fori_loop(0, CHUNKS, turn, 0)

    for copy in own_lead + lead_swaps:
        copy.wait()

    def lead_terms(c, _):
        rows = pl.ds(pl.multiple_of(c * 256, 256), 256)
        product = jnp.dot(image_t[rows, :], lead_window[...], preferred_element_type=F32)
        for i in range(16):
            value = product[i * 16 : i * 16 + 16, :]
            lead_home[c, i // 4, i % 4] = value
            lead_out[c, i // 4, i % 4] = value.astype(BF16)
        return 0

    lax.fori_loop(0, 4, lead_terms, 0)

    def fetch(rb):
        slot = rb % 2
        begin = pl.multiple_of(rb * 512 + core * 256, 256)
        return (
            pltpu.make_async_copy(
                basis.at[:, pl.ds(begin, 256)],
                window.at[slot, pl.ds(0, 512), :],
                load_sem.at[3 + slot],
            ),
            pltpu.make_async_copy(
                far(rb), window.at[slot, pl.ds(512, 512), :], load_sem.at[5 + slot]
            ),
        )

    def start_fetch(rb):
        swap(rb, far(rb)).wait()
        for copy in fetch(rb):
            copy.start()

    def multiply(rb, read):
        to_x, to_z = (rb % 2) * 2 + rb // 8, (rb // 2) % 4

        def one(c, _):
            rows = pl.ds(pl.multiple_of(c * 256, 256), 256)
            product = jnp.dot(image_t[rows, :], read(), preferred_element_type=F32)
            home[to_x, to_z, c] = product
            out[to_x, to_z, c] = product.astype(BF16)
            return 0

        lax.fori_loop(0, 4, one, 0)

    def terms(low, high):
        def one(rb, _):
            for copy in fetch(rb):
                copy.wait()

            @pl.when(rb < 15)
            def _():
                start_fetch(rb + 1)

            multiply(rb, lambda: window[rb % 2])
            return 0

        lax.fori_loop(low, high, one, 0)

    def lead_block(rb):
        multiply(rb, lambda: lead_window[:, rb * 256 : rb * 256 + 256])

    dims = [LEAD_ORDERS[p] for p in range(2)]
    homes, outs, lane = [lead_home] * 2, [lead_out] * 2, [0, 256]
    for stage in range(3):
        steps = [
            Reduce(
                place, wires, LEAD_ORDERS[p][stage], dims[p], homes[p], outs[p], EVERY, lane[p],
                lead_gots[p * 3 + stage], direct=stage > 0,
            )
            for p in range(2)
        ]
        for step in steps:
            step.begin()
        for step in steps:
            step.follow()
        if stage == 0:
            start_fetch(2)
            lead_block(0)
            lead_block(1)
        else:
            terms(5 * stage, 5 * stage + 2)
        for step in steps:
            step.relay()
        if stage == 0:
            terms(2, 5)
        else:
            terms(5 * stage + 2, 5 * stage + 5)
        for p, step in enumerate(steps):
            if stage < 2:
                acc = lead_sums[p * 2 + stage]

                def store(index, half, value, acc=acc):
                    acc[index + (EVERY, pl.ds(half * 128, 128))] = value

                homes[p] = outs[p] = acc
                lane[p] = 0
            else:
                at = [position(axis, place) for axis in LEAD_ORDERS[p]]
                rows = pl.ds(pl.multiple_of((at[0] * 16 + at[1] * 4 + at[2]) * 16, 16), 16)

                def store(index, half, value, p=p, rows=rows):
                    begin = pl.multiple_of(p * 512 + core * 256 + half * 128, 128)
                    work[rows, pl.ds(begin, 128)] = value

            step.finish(store)
            dims[p] = step.rest
    def gather_rows():
        step = Gather(
            place, wires, "y", rows_t, 0, 256, pl.ds(0, 256), [pl.ds(0, 128), pl.ds(128, 128)], relayed=True
        )
        step.begin()
        yield
        step.relay()
        yield
        step.pass_on()
        step.arrive()
        step.finish()

    mine = pl.ds(pl.multiple_of(gy * 128, 128), 128)
    theirs = pl.ds(pl.multiple_of((gy + 1 - 2 * core) * 128, 128), 128)
    lanes = pl.ds(pl.multiple_of(core * 256, 256), 256)

    def all_rows():
        dims, rows = [DIMS] * 3, [pl.ds(begin, size) for begin, size in PARTS]
        homes, outs = [home] * 3, [out] * 3
        for stage in range(3):
            steps = [
                Reduce(
                    place, wires, ORDERS[p][stage], dims[p], homes[p], outs[p], rows[p], 0,
                    gots[p * 3 + stage], loop=True, direct=stage == 2,
                )
                for p in range(3)
            ]
            for step in steps:
                step.begin()
            if stage == 0:
                yield
            for step in steps:
                step.follow()
            yield
            if stage < 2:
                for step in steps:
                    step.relay()
                yield
            for p, step in enumerate(steps):
                if stage < 2:
                    acc = sums[p * 2 + stage]

                    def store(index, half, value, acc=acc):
                        acc[index + (EVERY, pl.ds(half * 128, 128))] = value

                    homes[p] = outs[p] = acc
                    rows[p] = EVERY
                else:

                    def store(index, half, value, p=p):
                        begin = pl.multiple_of(y * 256 + PARTS[p][0], 16)
                        rows_t[pl.ds(begin, PARTS[p][1]), pl.ds(half * 128, 128)] = value

                step.finish(store)
                dims[p] = step.rest
        swapped = wires.send(wires.take(), rows_t.at[theirs, :], tile.at[:, lanes], mate)
        tile[:, lanes] = rows_t[mine, :]
        yield from gather_rows()
        swapped.wait()

    events = all_rows()

    for stage in range(3):
        steps = []
        for p in range(2):
            at = [position(axis, place) for axis in LEAD_ORDERS[p]]
            base = (at[0] * 256 + at[1] * 64, at[0] * 256, 0)[stage]
            begin = pl.multiple_of(p * 512 + core * 256, 256)
            halves = [pl.ds(begin, 128), pl.ds(pl.multiple_of(begin + 128, 128), 128)]
            steps.append(
                Gather(
                    place, wires, LEAD_ORDERS[p][2 - stage], work, base, (16, 64, 256)[stage],
                    pl.ds(begin, 256), halves, mate if stage == 2 else None,
                )
            )
        for step in steps:
            step.begin()
        if stage == 0:
            terms(15, 16)
        for _ in range(AHEAD[2 * stage]):
            next(events)
        for step in steps:
            step.relay()
        for step in steps:
            step.pass_on()
        for _ in range(AHEAD[2 * stage + 1]):
            next(events)
        if stage < 2:
            for step in steps:
                step.arrive()
                step.finish()

    for step in steps:
        step.arrive()
    for step in steps:
        step.finish()
    for b in range(0, COLS, NB):
        block = work[b : b + NB, b : b + NB]
        work[b : b + NB, b : b + NB] = 0.5 * (block + block.T)
    count = [0]

    def between(_):
        if count[0] in WHEN:
            next(events)
        count[0] += 1

    invert_factor(work, a_ref, x_ref, between)
    for _ in events:
        pass
    last = None
    for columns, side in ((theirs, gy + 1 - 2 * core), (mine, gy)):
        block = work[columns, :]
        lane = lax.broadcasted_iota(jnp.int32, block.shape, 1)
        block = jnp.where(lane < (side + 1) * 128, block, 0.0)
        value = dot_two(block, rows_t[...])
        column = side * 128 + lax.broadcasted_iota(jnp.int32, value.shape, 0)
        row = (gx * 2 + gz) * 512 + core * 256 + lax.broadcasted_iota(jnp.int32, value.shape, 1)
        value = jnp.where(column <= row, value, 0.0)
        if last is None:
            total[...] = value
            last = wires.send(wires.take(), total, factor.at[:, lanes], mate)
        else:
            factor[:, lanes] = value
    last.wait()


AHEAD = (1, 0, 1, 0, 0, 1)
WHEN = (26, 46, 72, 90, 108)
WIRES = 200


def project(basis, classes, cond_table, ground_table, port_cells, port_load):
    any_spec = pl.BlockSpec(memory_space=pltpu.HBM)
    vmem = pl.BlockSpec(memory_space=pltpu.VMEM)
    smem = pl.BlockSpec(memory_space=pltpu.SMEM)
    lead_gots, lead_sums, gots, sums = [], [], [], []
    for _ in range(2):
        lead_gots += [
            pltpu.VMEM((6, 4, 4, 16, 128), BF16),
            pltpu.VMEM((6, 4, 16, 128), F32),
            pltpu.VMEM((6, 16, 128), F32),
        ]
        lead_sums += [pltpu.VMEM((4, 4, 16, 256), F32), pltpu.VMEM((4, 16, 256), F32)]
    for _, size in PARTS:
        gots += [
            pltpu.VMEM((6, 4, 4, size, 128), BF16),
            pltpu.VMEM((6, 4, size, 128), F32),
            pltpu.VMEM((6, size, 128), F32),
        ]
        sums += [pltpu.VMEM((4, 4, size, 256), F32), pltpu.VMEM((4, size, 256), F32)]
    return pl.pallas_call(
        kernel,
        out_shape=(
            jax.ShapeDtypeStruct((128, 512), F32),
            jax.ShapeDtypeStruct((128, 512), F32),
            jax.ShapeDtypeStruct((512, 4096), BF16),
        ),
        in_specs=[any_spec, vmem, smem, smem, vmem, vmem],
        out_specs=(vmem, vmem, any_spec),
        scratch_shapes=[
            pltpu.VMEM((512, 128), F32),
            pltpu.VMEM((512, 128), F32),
            pltpu.VMEM((512, COLS), BF16),
            pltpu.VMEM((512, COLS), BF16),
            pltpu.VMEM((5, 64, COLS), BF16),
            pltpu.VMEM((5, 64, COLS), BF16),
            pltpu.VMEM((64, 128), F32),
            pltpu.VMEM((1024, COLS), BF16),
            pltpu.VMEM((COLS, 1024), BF16),
            pltpu.VMEM((1024, 512), BF16),
            pltpu.VMEM((4, 4, 4, 16, 512), F32),
            pltpu.VMEM((4, 4, 4, 16, 512), BF16),
            pltpu.VMEM((2, 1024, 256), BF16),
            pltpu.VMEM((4, 4, 4, 256, 256), F32),
            pltpu.VMEM((4, 4, 4, 256, 256), BF16),
            pltpu.VMEM((COLS, COLS), F32),
            pltpu.VMEM((128, 128), F32),
            pltpu.VMEM((128, 128), F32),
            pltpu.VMEM((128, 256), F32),
            pltpu.VMEM((COLS, 256), F32),
            *lead_gots,
            *lead_sums,
            *gots,
            *sums,
            pltpu.SemaphoreType.DMA((7,)),
            pltpu.SemaphoreType.DMA((WIRES,)),
            pltpu.SemaphoreType.DMA((WIRES,)),
        ],
        compiler_params=pltpu.CompilerParams(
            collective_id=0, has_side_effects=True, vmem_limit_bytes=67043328
        ),
        name="project",
    )(basis, classes, cond_table, ground_table, port_cells, port_load)


def turn_kernel(tile, factor, tile_out, factor_out):
    tile_out[...] = tile[...].T
    factor_out[...] = factor[...].T


def local(basis, classes, cond_table, ground_table, port_cells, port_load):
    flat = basis.reshape(512, basis.shape[3])
    tile, factor, _ = project(
        flat, classes, cond_table, ground_table, port_cells.reshape(16, 128), port_load.reshape(16, 128)
    )
    shape = jax.ShapeDtypeStruct((512, 128), F32)
    return pl.pallas_call(turn_kernel, out_shape=(shape, shape), name="turn")(tile, factor)


def solution(mesh):
    placed = (P("gx", "gy", "gz", None), P("gx", "gy", "gz"), P(), P(), P(), P())
    return jax.shard_map(
        local,
        mesh=mesh,
        in_specs=placed,
        out_specs=(P(("gx", "gz"), "gy"), P(("gx", "gz"), "gy")),
        check_vma=False,
    )
```

```python
import jax
import jax.numpy as jnp
from jax import lax
from jax.experimental import pallas as pl
from jax.experimental.pallas import tpu as pltpu
from jax.sharding import PartitionSpec as P

NB = 512
PANELS = 2
COLS = NB * PANELS
F32 = jnp.float32
BF16 = jnp.bfloat16
MESH = pl.DeviceIdType.MESH
EVERY = slice(None)


def here():
    gx, gy, gz = lax.axis_index("gx"), lax.axis_index("gy"), lax.axis_index("gz")
    return gz * 2 + gx // 4, gy // 2, gx % 4, gy % 2


def device(x, y, z, core):
    return ((x % 2) * 4 + z, y * 2 + core, x // 2)


def along(axis, pos, place):
    x, y, z, core = place
    if axis == "x":
        x = pos
    elif axis == "y":
        y = pos
    else:
        z = pos
    return device(x, y, z, core)


def position(axis, place):
    return place["xyz".index(axis)]


def greet(devices):
    barrier = pltpu.get_barrier_semaphore()
    for dev in devices:
        pl.semaphore_signal(barrier, inc=1, device_id=dev, device_id_type=MESH)
    pl.semaphore_wait(barrier, len(devices))


def torus_peers(place):
    x, y, z, core = place
    peers = []
    for axis in "xyz":
        pos = position(axis, place)
        peers += [along(axis, (pos + d) % 4, place) for d in (1, 2, 3)]
    return peers + [device(x, y, z, 1 - core)]


class Wires:
    def __init__(self, send_sem, recv_sem):
        self.send_sem, self.recv_sem, self.used = send_sem, recv_sem, 0

    def take(self, count=1):
        self.used += count
        return self.used - count

    def copy(self, number, src, dst, dev):
        return pltpu.make_async_remote_copy(
            src_ref=src,
            dst_ref=dst,
            send_sem=self.send_sem.at[number],
            recv_sem=self.recv_sem.at[number],
            device_id=dev,
            device_id_type=MESH,
        )

    def send(self, number, src, dst, dev):
        copy = self.copy(number, src, dst, dev)
        copy.start()
        return copy


def each(dims, body, loop):
    if not loop or len(dims) < 2:
        body((EVERY,) * len(dims))
        return

    def step(i, _):
        body((i,) + (EVERY,) * (len(dims) - 1))
        return 0

    lax.fori_loop(0, 4, step, 0)


def put(index, dims, axis, pos):
    index = list(index)
    index.insert(dims.index(axis), pos)
    return tuple(index)


class Reduce:
    def __init__(
        self, place, wires, axis, dims, home, out, rows, lane, got, loop=False, direct=False
    ):
        self.axis, self.dims, self.home, self.out, self.rows, self.got = axis, dims, home, out, rows, got
        self.loop, self.direct = loop, direct
        self.across = along(axis, (position(axis, place) + 2) % 4, place)
        self.first, self.second = pl.ds(lane, 128), pl.ds(lane + 128, 128)
        self.rest = tuple(d for d in dims if d != axis)
        self.wires, self.base = wires, wires.take(6)
        me = position(axis, place)
        self.me, self.plus, self.minus, self.opposite = me, (me + 1) % 4, (me + 3) % 4, (me + 2) % 4
        self.up, self.down = along(axis, self.plus, place), along(axis, self.minus, place)
        self.copies = {}

    def go(self, slot, pos, lanes, dev):
        index = put([pl.ds(0, 4)] * len(self.rest), self.dims, self.axis, pos)
        src = self.out.at[index + (self.rows, lanes)]
        self.copies[slot] = self.wires.send(self.base + slot, src, self.got.at[slot], dev)

    def begin(self):
        self.go(0, self.opposite, self.first, self.across if self.direct else self.up)
        self.go(3, self.opposite, self.second, self.across if self.direct else self.down)

    def follow(self):
        self.go(1, self.plus, self.second, self.up)
        self.go(4, self.minus, self.first, self.down)
        if self.direct:
            self.go(2, self.plus, self.first, self.up)
            self.go(5, self.minus, self.second, self.down)

    def relay(self):
        if self.direct:
            return
        for slot, pos, lanes, dev in (
            (0, self.plus, self.first, self.up),
            (3, self.minus, self.second, self.down),
        ):
            self.copies[slot].wait_recv()

            def body(index):
                at = put(index, self.dims, self.axis, pos) + (self.rows, lanes)
                total = self.home[at] + self.got[(slot,) + index].astype(F32)
                self.out[at] = total.astype(self.out.dtype)

            each(self.rest, body, self.loop)
            self.go(slot + 2, pos, lanes, dev)

    def finish(self, store):
        self.collect(store)
        self.drain()

    def collect(self, store):
        for slot in (1, 4, 2, 5) + ((0, 3) if self.direct else ()):
            self.copies[slot].wait_recv()

        def body(index):
            for half, lanes, one, two in ((0, self.first, 2, 4), (1, self.second, 1, 5)):
                at = put(index, self.dims, self.axis, self.me) + (self.rows, lanes)
                total = self.home[at] + self.got[(one,) + index].astype(F32)
                total = total + self.got[(two,) + index].astype(F32)
                if self.direct:
                    total = total + self.got[(3 * half,) + index].astype(F32)
                store(index, half, total)

        each(self.rest, body, self.loop)

    def drain(self):
        for copy in self.copies.values():
            copy.wait_send()


class Gather:
    def __init__(self, place, wires, axis, ref, base, size, lanes, halves, mate=None, relayed=False):
        self.ref, self.base, self.size, self.mate = ref, base, size, mate
        self.lanes, self.halves = lanes, halves
        self.wires, self.first = wires, wires.take(10)
        me = position(axis, place)
        self.me, self.plus, self.minus, self.opposite = me, (me + 1) % 4, (me + 3) % 4, (me + 2) % 4
        self.up, self.down = along(axis, self.plus, place), along(axis, self.minus, place)
        self.across = along(axis, self.opposite, place)
        self.direct = mate is None and not relayed
        self.copies = []
        self.passed = []

    def go(self, slot, pos, lanes, dev):
        rows = pl.ds(pl.multiple_of(self.base + pos * self.size, self.size), self.size)
        part = self.ref.at[rows, lanes]
        return self.wires.send(self.first + slot, part, part, dev)

    def share(self, slot, pos):
        if self.mate is not None:
            self.passed.append(self.go(slot, pos, self.lanes, self.mate))

    def begin(self):
        if self.direct:
            for slot, dev in enumerate((self.across, self.up, self.down)):
                self.copies += [self.go(slot, self.me, self.lanes, dev)]
            return
        low, high = self.halves
        self.copies += [self.go(0, self.me, low, self.up), self.go(1, self.me, high, self.down)]
        self.copies += [self.go(8, self.me, high, self.up), self.go(9, self.me, low, self.down)]
        self.share(4, self.me)

    def relay(self):
        if self.direct:
            return
        low, high = self.halves
        self.copies[0].wait_recv()
        self.copies += [self.go(2, self.minus, low, self.up)]
        self.copies[1].wait_recv()
        self.copies += [self.go(3, self.plus, high, self.down)]

    def pass_on(self):
        if self.direct:
            return
        self.copies[2].wait_recv()
        self.copies[3].wait_recv()
        self.share(5, self.minus)
        self.share(6, self.plus)

    def arrive(self):
        if self.direct:
            for copy in self.copies:
                copy.wait_recv()
            return
        self.copies[4].wait_recv()
        self.copies[5].wait_recv()
        self.share(7, self.opposite)

    def finish(self):
        for copy in self.passed:
            copy.wait_recv()
        for copy in self.copies + self.passed:
            copy.wait_send()


def row_of(block, k):
    return jnp.broadcast_to(block[k : k + 1, :], block.shape)


def pieces(value, count):
    terms = []
    for _ in range(count):
        term = value.astype(BF16).astype(F32)
        terms.append(term)
        value = value - term
    return terms


def eliminate(rows, right, cols, sub):
    scale = jnp.zeros((8, 128), F32)
    for k in range(8):
        inv = 1.0 / row_of(cols[0][k], k)
        scale = jnp.where(sub == k, inv, scale)
        pivot_row = row_of(rows[0], k)
        pivot_right = row_of(right[0], k)
        heads = [row_of(cols[0][m], k) for m in range(k + 1, 8)]
        for t in range(len(rows)):
            mult = cols[t][k] * inv
            if t == 0:
                mult = jnp.where(sub > k, mult, 0.0)
            for i, m in enumerate(range(k + 1, 8)):
                cols[t][m] = cols[t][m] - mult * heads[i]
            rows[t] = rows[t] - mult * pivot_row
            right[t] = right[t] - mult * pivot_right
    return rows, right, scale


def stack_dot(left, right):
    a1, a2, a3 = pieces(left, 3)
    b1, b2, b3 = pieces(right, 3)
    a = jnp.concatenate([a1, a1, a2, a2, a1, a3], axis=0).astype(BF16)
    b = jnp.concatenate([b1, b2, b1, b2, b3, b1], axis=0).astype(BF16)
    return lax.dot_general(a, b, (((0,), (0,)), ((), ())), preferred_element_type=F32)


def factor_block(a_ref, x_ref, middle):
    sub = lax.broadcasted_iota(jnp.int32, (8, 128), 0)
    row = lax.broadcasted_iota(jnp.int32, (128, 128), 0)
    lane = lax.broadcasted_iota(jnp.int32, (128, 128), 1)
    x_ref[...] = jnp.where(row == lane, 1.0, 0.0).astype(F32)
    for g in range(16):
        b = g * 8
        n = 2 if g < 15 else 1
        rows = [a_ref[b + 8 * t : b + 8 * t + 8, :] for t in range(n)]
        right = [x_ref[b + 8 * t : b + 8 * t + 8, :] for t in range(n)]
        cols = [
            [jnp.broadcast_to(rows[t][:, b + m : b + m + 1], (8, 128)) for m in range(8)]
            for t in range(n)
        ]
        rows, right, scale = eliminate(rows, right, cols, sub)
        if n == 2:
            a_ref[b + 8 : b + 16, :] = rows[1]
            x_ref[b + 8 : b + 16, :] = right[1]
        if g < 14:
            low = b + 16
            both = jnp.concatenate([rows[0], right[0]], axis=1)
            change = stack_dot(rows[0] * scale, both)
            a_ref[low:, :] = a_ref[low:, :] - change[low:, :128]
            x_ref[low:, :] = x_ref[low:, :] - change[low:, 128:]
        x_ref[b : b + 8, :] = right[0] * jnp.sqrt(scale)
        middle(g)


def two(value):
    high = value.astype(BF16)
    return high, (value - high.astype(F32)).astype(BF16)


def dot_two(left, right):
    lh, ll = two(left)
    rh, rl = two(right)
    return jnp.dot(
        jnp.concatenate([lh, ll, lh], axis=1),
        jnp.concatenate([rh, rh, rl], axis=0),
        preferred_element_type=F32,
    )


def invert_factor(work, a_ref, x_ref, between):
    n = work.shape[0]
    for k in range(n // 128):
        b, e = k * 128, k * 128 + 128
        a_ref[...] = work[b:e, b:e]
        factor_block(a_ref, x_ref, between)
        inverse = x_ref[...]
        for low, high in ((0, b), (e, n)):
            if low < high:
                work[b:e, low:high] = dot_two(inverse, work[b:e, low:high])
        work[b:e, b:e] = inverse
        if e < n:
            high, low = two(work[b:e, :])
            left = jnp.concatenate([high[:, e:], low[:, e:], high[:, e:]], axis=0)
            both = jnp.concatenate([high, high, low], axis=0)
            change = lax.dot_general(
                left, both, (((0,), (0,)), ((), ())), preferred_element_type=F32
            )
            if b:
                work[e:, :b] = work[e:, :b] - change[:, :b]
            work[e:, b:e] = -change[:, b:e]
            work[e:, e:] = work[e:, e:] - change[:, e:]
        between(16)


DIMS = "xzy"
ORDERS = ("xyz", "yzx", "zxy")
LEAD_ORDERS = ("xyz", "yzx")
PARTS = ((0, 96), (96, 80), (176, 80))
CHUNKS = COLS // 128


def kernel(
    basis, classes, cond_table, ground_table, port_cells, port_load, tile, factor, other,
    cond, ground, panel, scaled, faces, halos, hz, image, image_t,
    lead_window, lead_home, lead_out, window, home, out, work, a_ref, x_ref, total, rows_t,
    *rest,
):
    lead_gots, lead_sums, gots, sums = rest[:6], rest[6:10], rest[10:19], rest[19:25]
    load_sem, send_sem, recv_sem = rest[25:]
    wires = Wires(send_sem, recv_sem)
    gx, gy, gz = lax.axis_index("gx"), lax.axis_index("gy"), lax.axis_index("gz")
    place = here()
    x, y, z, core = place
    mate = device(x, y, z, 1 - core)
    beside = [
        ((gx + 7) % 8, gy, gz),
        ((gx + 1) % 8, gy, gz),
        (gx, (gy + 7) % 8, gz),
        (gx, (gy + 1) % 8, gz),
        (gx, gy, 1 - gz),
    ]
    load = pltpu.make_async_copy(basis.at[:, pl.ds(0, COLS)], panel, load_sem.at[0])
    load.start()
    own_lead = []
    for rb in range(2):
        begin = pl.multiple_of(rb * 512 + core * 256, 256)
        own_lead.append(
            pltpu.make_async_copy(
                basis.at[:, pl.ds(begin, 256)],
                lead_window.at[pl.ds(0, 512), pl.ds(rb * 256, 256)],
                load_sem.at[1 + rb],
            )
        )
        own_lead[rb].start()
    greet(beside + torus_peers(place))

    swap_base = wires.take(16)

    def swap(rb, dst):
        begin = pl.multiple_of(rb * 512 + (1 - core) * 256, 256)
        return wires.copy(swap_base + rb, basis.at[:, pl.ds(begin, 256)], dst, mate)

    def far(rb):
        return other.at[:, pl.ds(pl.multiple_of(rb * 256, 256), 256)]

    lead_swaps = [
        swap(rb, lead_window.at[pl.ds(512, 512), pl.ds(rb * 256, 256)]) for rb in range(2)
    ]
    for copy in lead_swaps:
        copy.start()

    def look_up(i, _):
        kinds = classes[i]
        lane = lax.broadcasted_iota(jnp.int32, (8, 8), 1)
        diagonal = lane == lax.broadcasted_iota(jnp.int32, (8, 8), 0)
        for table, out_ref in ((cond_table, cond), (ground_table, ground)):
            values = jnp.zeros((8, 8), F32)
            for kind in range(16):
                values = jnp.where(kinds == kind, table[kind], values)
            columns = []
            for j in range(8):
                line = jnp.broadcast_to(values[j : j + 1, :], (8, 8))
                line = jnp.sum(jnp.where(diagonal, line, 0.0), axis=1, keepdims=True)
                columns.append(jnp.broadcast_to(line, (8, 128)))
            rows = pl.ds(pl.multiple_of(i * 64, 64), 64)
            out_ref[rows, :] = jnp.concatenate(columns, axis=0)
        return 0

    lax.fori_loop(0, 8, look_up, 0)
    load.wait()

    def scale(c, _):
        lanes = pl.ds(pl.multiple_of(c * 128, 128), 128)
        inner = lax.broadcasted_iota(jnp.int32, (8, 128), 0)
        y_low, y_high, z_face = [], [], []
        for i in range(8):
            rows = pl.ds(i * 64, 64)
            value = (cond[rows, :] * panel[rows, lanes].astype(F32)).astype(BF16)
            scaled[rows, lanes] = value
            if i == 0:
                faces[0, :, lanes] = value
            if i == 7:
                faces[1, :, lanes] = value
            value = value.astype(F32)
            y_low.append(value[:8])
            y_high.append(value[56:])
            face = jnp.zeros((8, 128), F32)
            for j in range(8):
                cell = value[j * 8 : j * 8 + 8]
                low = jnp.broadcast_to(cell[0:1, :], (8, 128))
                high = jnp.broadcast_to(cell[7:8, :], (8, 128))
                face = jnp.where(inner == j, jnp.where(gz == 1, low, high), face)
            z_face.append(face)
        for f, face in ((2, y_low), (3, y_high), (4, z_face)):
            faces[f, :, lanes] = jnp.concatenate(face, axis=0).astype(BF16)
        return 0

    lax.fori_loop(0, CHUNKS, scale, 0)
    lands = [1, 0, 3, 2, 4]
    face_base = wires.take(5)
    face_copies = [
        wires.send(face_base + f, faces.at[f], halos.at[lands[f]], beside[f]) for f in range(5)
    ]

    def start_swap(rb, _):
        swap(rb, far(rb)).start()
        return 0

    lax.fori_loop(2, 16, start_swap, 0)
    def add_ports(i, _):
        row = lax.broadcasted_iota(jnp.int32, (64, 128), 0)
        flat = ((gx * 8 + i) * 64 + gy * 8 + row // 8) * 16 + gz * 8 + row % 8
        found = jnp.zeros((64, 128), F32)
        for j in range(16):
            match = flat == jnp.broadcast_to(port_cells[j : j + 1, :], (64, 128))
            found = found + jnp.where(match, jnp.broadcast_to(port_load[j : j + 1, :], (64, 128)), 0.0)
        rows = pl.ds(pl.multiple_of(i * 64, 64), 64)
        ground[rows, :] = ground[rows, :] + jnp.sum(found, axis=1, keepdims=True)
        return 0

    lax.fori_loop(0, 8, add_ports, 0)
    for copy in face_copies:
        copy.wait()

    keep = [gx > 0, gx < 7, gy > 0, gy < 7]
    image_base = wires.take(CHUNKS)

    def image_copy(c):
        lanes = pl.ds(pl.multiple_of(c * 128, 128), 128)
        return wires.copy(
            image_base + c, image.at[pl.ds(0, 512), lanes], image.at[pl.ds(512, 512), lanes], mate
        )

    def stencil(c, _):
        lanes = pl.ds(pl.multiple_of(c * 128, 128), 128)
        inner = lax.broadcasted_iota(jnp.int32, (64, 128), 0) % 8

        def halo(f):
            return jnp.where(keep[f], halos[f, :, lanes].astype(F32), 0.0)

        hz[...] = halos[4, :, lanes].astype(F32)
        x_low, x_high, y_low, y_high = halo(0), halo(1), halo(2), halo(3)
        for i in range(8):
            rows = pl.ds(i * 64, 64)
            me = scaled[rows, lanes].astype(F32)
            down = scaled[pl.ds((i - 1) * 64, 64), lanes].astype(F32) if i > 0 else x_low
            up = scaled[pl.ds((i + 1) * 64, 64), lanes].astype(F32) if i < 7 else x_high
            around = up + down
            around = around + jnp.concatenate([me[8:], y_high[i * 8 : i * 8 + 8]], axis=0)
            around = around + jnp.concatenate([y_low[i * 8 : i * 8 + 8], me[:56]], axis=0)
            ends = jnp.concatenate(
                [jnp.broadcast_to(hz[i * 8 + j : i * 8 + j + 1, :], (8, 128)) for j in range(8)],
                axis=0,
            )
            high = pltpu.roll(me, 63, 0)
            low = pltpu.roll(me, 1, 0)
            high = jnp.where(inner == 7, jnp.where(gz == 0, ends, 0.0), high)
            low = jnp.where(inner == 0, jnp.where(gz == 1, ends, 0.0), low)
            around = around + high + low
            value = cond[rows, :] * (6.0 * me - around)
            value = value + ground[rows, :] * panel[rows, lanes].astype(F32)
            image[rows, lanes] = value.astype(BF16)
        image_copy(c).start()
        return 0

    lax.fori_loop(0, CHUNKS, stencil, 0)

    def turn(c, _):
        image_copy(c).wait()
        rows = pl.ds(pl.multiple_of(c * 128, 128), 128)
        image_t[rows, :] = image[:, rows].T
        return 0

    lax.fori_loop(0, CHUNKS, turn, 0)

    for copy in own_lead + lead_swaps:
        copy.wait()

    def lead_terms(c, _):
        rows = pl.ds(pl.multiple_of(c * 256, 256), 256)
        product = jnp.dot(image_t[rows, :], lead_window[...], preferred_element_type=F32)
        for i in range(16):
            value = product[i * 16 : i * 16 + 16, :]
            lead_home[c, i // 4, i % 4] = value
            lead_out[c, i // 4, i % 4] = value.astype(BF16)
        return 0

    lax.fori_loop(0, 4, lead_terms, 0)

    def fetch(rb):
        slot = rb % 2
        begin = pl.multiple_of(rb * 512 + core * 256, 256)
        return (
            pltpu.make_async_copy(
                basis.at[:, pl.ds(begin, 256)],
                window.at[slot, pl.ds(0, 512), :],
                load_sem.at[3 + slot],
            ),
            pltpu.make_async_copy(
                far(rb), window.at[slot, pl.ds(512, 512), :], load_sem.at[5 + slot]
            ),
        )

    def start_fetch(rb):
        swap(rb, far(rb)).wait()
        for copy in fetch(rb):
            copy.start()

    def multiply(rb, read):
        to_x, to_z = (rb % 2) * 2 + rb // 8, (rb // 2) % 4

        def one(c, _):
            rows = pl.ds(pl.multiple_of(c * 256, 256), 256)
            product = jnp.dot(image_t[rows, :], read(), preferred_element_type=F32)
            home[to_x, to_z, c] = product
            out[to_x, to_z, c] = product.astype(BF16)
            return 0

        lax.fori_loop(0, 4, one, 0)

    def terms(low, high):
        def one(rb, _):
            for copy in fetch(rb):
                copy.wait()

            @pl.when(rb < 15)
            def _():
                start_fetch(rb + 1)

            multiply(rb, lambda: window[rb % 2])
            return 0

        lax.fori_loop(low, high, one, 0)

    def lead_block(rb):
        multiply(rb, lambda: lead_window[:, rb * 256 : rb * 256 + 256])

    dims = [LEAD_ORDERS[p] for p in range(2)]
    homes, outs, lane = [lead_home] * 2, [lead_out] * 2, [0, 256]
    for stage in range(3):
        steps = [
            Reduce(
                place, wires, LEAD_ORDERS[p][stage], dims[p], homes[p], outs[p], EVERY, lane[p],
                lead_gots[p * 3 + stage], direct=stage > 0,
            )
            for p in range(2)
        ]
        for step in steps:
            step.begin()
        for step in steps:
            step.follow()
        if stage == 0:
            start_fetch(2)
            lead_block(0)
            lead_block(1)
        else:
            terms(5 * stage, 5 * stage + 2)
        for step in steps:
            step.relay()
        if stage == 0:
            terms(2, 5)
        else:
            terms(5 * stage + 2, 5 * stage + 5)
        for p, step in enumerate(steps):
            if stage < 2:
                acc = lead_sums[p * 2 + stage]

                def store(index, half, value, acc=acc):
                    acc[index + (EVERY, pl.ds(half * 128, 128))] = value

                homes[p] = outs[p] = acc
                lane[p] = 0
            else:
                at = [position(axis, place) for axis in LEAD_ORDERS[p]]
                rows = pl.ds(pl.multiple_of((at[0] * 16 + at[1] * 4 + at[2]) * 16, 16), 16)

                def store(index, half, value, p=p, rows=rows):
                    begin = pl.multiple_of(p * 512 + core * 256 + half * 128, 128)
                    work[rows, pl.ds(begin, 128)] = value

            step.finish(store)
            dims[p] = step.rest
    def gather_rows():
        step = Gather(
            place, wires, "y", rows_t, 0, 256, pl.ds(0, 256), [pl.ds(0, 128), pl.ds(128, 128)], relayed=True
        )
        step.begin()
        yield
        step.relay()
        yield
        step.pass_on()
        step.arrive()
        step.finish()

    mine = pl.ds(pl.multiple_of(gy * 128, 128), 128)
    theirs = pl.ds(pl.multiple_of((gy + 1 - 2 * core) * 128, 128), 128)
    lanes = pl.ds(pl.multiple_of(core * 256, 256), 256)

    def all_rows():
        def make(p, stage, dims, terms_ref, sent_ref, rows):
            return Reduce(
                place, wires, ORDERS[p][stage], dims, terms_ref, sent_ref, rows, 0,
                gots[p * 3 + stage], loop=True, direct=stage == 2,
            )

        steps = [make(p, 0, DIMS, home, out, pl.ds(*PARTS[p])) for p in range(3)]
        for step in steps:
            step.begin()
        yield
        for step in steps:
            step.follow()
        yield
        for stage in range(2):
            for step in steps:
                step.relay()
            yield
            later = []
            for p, step in enumerate(steps):
                acc = sums[p * 2 + stage]

                def store(index, half, value, acc=acc):
                    acc[index + (EVERY, pl.ds(half * 128, 128))] = value

                step.collect(store)
                later.append(make(p, stage + 1, step.rest, acc, acc, EVERY))
                later[p].begin()
                later[p].follow()
            for step in steps:
                step.drain()
            steps = later
            yield
        for p, step in enumerate(steps):

            def store(index, half, value, p=p):
                begin = pl.multiple_of(y * 256 + PARTS[p][0], 16)
                rows_t[pl.ds(begin, PARTS[p][1]), pl.ds(half * 128, 128)] = value

            step.finish(store)
        swapped = wires.send(wires.take(), rows_t.at[theirs, :], tile.at[:, lanes], mate)
        tile[:, lanes] = rows_t[mine, :]
        yield from gather_rows()
        swapped.wait()

    events = all_rows()

    for stage in range(3):
        steps = []
        for p in range(2):
            at = [position(axis, place) for axis in LEAD_ORDERS[p]]
            base = (at[0] * 256 + at[1] * 64, at[0] * 256, 0)[stage]
            begin = pl.multiple_of(p * 512 + core * 256, 256)
            halves = [pl.ds(begin, 128), pl.ds(pl.multiple_of(begin + 128, 128), 128)]
            steps.append(
                Gather(
                    place, wires, LEAD_ORDERS[p][2 - stage], work, base, (16, 64, 256)[stage],
                    pl.ds(begin, 256), halves, mate if stage == 2 else None,
                )
            )
        for step in steps:
            step.begin()
        if stage == 0:
            terms(15, 16)
        for _ in range(AHEAD[2 * stage]):
            next(events)
        for step in steps:
            step.relay()
        for step in steps:
            step.pass_on()
        for _ in range(AHEAD[2 * stage + 1]):
            next(events)
        if stage < 2:
            for step in steps:
                step.arrive()
                step.finish()

    for step in steps:
        step.arrive()
    for step in steps:
        step.finish()
    for b in range(0, COLS, NB):
        block = work[b : b + NB, b : b + NB]
        work[b : b + NB, b : b + NB] = 0.5 * (block + block.T)
    count = [0]

    def between(_):
        if count[0] in WHEN:
            next(events)
        count[0] += 1

    invert_factor(work, a_ref, x_ref, between)
    for _ in events:
        pass
    last = None
    for columns, side in ((theirs, gy + 1 - 2 * core), (mine, gy)):
        block = work[columns, :]
        lane = lax.broadcasted_iota(jnp.int32, block.shape, 1)
        block = jnp.where(lane < (side + 1) * 128, block, 0.0)
        value = dot_two(block, rows_t[...])
        column = side * 128 + lax.broadcasted_iota(jnp.int32, value.shape, 0)
        row = (gx * 2 + gz) * 512 + core * 256 + lax.broadcasted_iota(jnp.int32, value.shape, 1)
        value = jnp.where(column <= row, value, 0.0)
        if last is None:
            total[...] = value
            last = wires.send(wires.take(), total, factor.at[:, lanes], mate)
        else:
            factor[:, lanes] = value
    last.wait()


AHEAD = (1, 0, 1, 0, 0, 1)
WHEN = (26, 46, 72, 90, 108)
WIRES = 200


def project(basis, classes, cond_table, ground_table, port_cells, port_load):
    any_spec = pl.BlockSpec(memory_space=pltpu.HBM)
    vmem = pl.BlockSpec(memory_space=pltpu.VMEM)
    smem = pl.BlockSpec(memory_space=pltpu.SMEM)
    lead_gots, lead_sums, gots, sums = [], [], [], []
    for _ in range(2):
        lead_gots += [
            pltpu.VMEM((6, 4, 4, 16, 128), BF16),
            pltpu.VMEM((6, 4, 16, 128), F32),
            pltpu.VMEM((6, 16, 128), F32),
        ]
        lead_sums += [pltpu.VMEM((4, 4, 16, 256), F32), pltpu.VMEM((4, 16, 256), F32)]
    for _, size in PARTS:
        gots += [
            pltpu.VMEM((6, 4, 4, size, 128), BF16),
            pltpu.VMEM((6, 4, size, 128), F32),
            pltpu.VMEM((6, size, 128), F32),
        ]
        sums += [pltpu.VMEM((4, 4, size, 256), F32), pltpu.VMEM((4, size, 256), F32)]
    return pl.pallas_call(
        kernel,
        out_shape=(
            jax.ShapeDtypeStruct((128, 512), F32),
            jax.ShapeDtypeStruct((128, 512), F32),
            jax.ShapeDtypeStruct((512, 4096), BF16),
        ),
        in_specs=[any_spec, vmem, smem, smem, vmem, vmem],
        out_specs=(vmem, vmem, any_spec),
        scratch_shapes=[
            pltpu.VMEM((512, 128), F32),
            pltpu.VMEM((512, 128), F32),
            pltpu.VMEM((512, COLS), BF16),
            pltpu.VMEM((512, COLS), BF16),
            pltpu.VMEM((5, 64, COLS), BF16),
            pltpu.VMEM((5, 64, COLS), BF16),
            pltpu.VMEM((64, 128), F32),
            pltpu.VMEM((1024, COLS), BF16),
            pltpu.VMEM((COLS, 1024), BF16),
            pltpu.VMEM((1024, 512), BF16),
            pltpu.VMEM((4, 4, 4, 16, 512), F32),
            pltpu.VMEM((4, 4, 4, 16, 512), BF16),
            pltpu.VMEM((2, 1024, 256), BF16),
            pltpu.VMEM((4, 4, 4, 256, 256), F32),
            pltpu.VMEM((4, 4, 4, 256, 256), BF16),
            pltpu.VMEM((COLS, COLS), F32),
            pltpu.VMEM((128, 128), F32),
            pltpu.VMEM((128, 128), F32),
            pltpu.VMEM((128, 256), F32),
            pltpu.VMEM((COLS, 256), F32),
            *lead_gots,
            *lead_sums,
            *gots,
            *sums,
            pltpu.SemaphoreType.DMA((7,)),
            pltpu.SemaphoreType.DMA((WIRES,)),
            pltpu.SemaphoreType.DMA((WIRES,)),
        ],
        compiler_params=pltpu.CompilerParams(
            collective_id=0, has_side_effects=True, vmem_limit_bytes=67043328
        ),
        name="project",
    )(basis, classes, cond_table, ground_table, port_cells, port_load)


def turn_kernel(tile, factor, tile_out, factor_out):
    tile_out[...] = tile[...].T
    factor_out[...] = factor[...].T


def local(basis, classes, cond_table, ground_table, port_cells, port_load):
    flat = basis.reshape(512, basis.shape[3])
    tile, factor, _ = project(
        flat, classes, cond_table, ground_table, port_cells.reshape(16, 128), port_load.reshape(16, 128)
    )
    shape = jax.ShapeDtypeStruct((512, 128), F32)
    return pl.pallas_call(turn_kernel, out_shape=(shape, shape), name="turn")(tile, factor)


def solution(mesh):
    placed = (P("gx", "gy", "gz", None), P("gx", "gy", "gz"), P(), P(), P(), P())
    return jax.shard_map(
        local,
        mesh=mesh,
        in_specs=placed,
        out_specs=(P(("gx", "gz"), "gy"), P(("gx", "gz"), "gy")),
        check_vma=False,
    )
```
